32 devices in a mesh: gx: 4 (over y, x), gy: 8 (over z, core).
Axes of the slice: x: 2, y: 2, z: 4, core: 2. Of those that a mesh axis runs over, the one named last changes fastest.
Arguments:
- grid_latent: bfloat16 [16384, 512], P(('gx', 'gy')), may hold values from -6 to 6
- mesh_latent: bfloat16 [4096, 512], P(('gx', 'gy')), may hold values from -6 to 6
- encode_senders: int32 [32, 4096], P(None, ('gx', 'gy')), may hold values from -1 to 16383, as said below
- mesh_senders: int32 [32, 4096], P(None, ('gx', 'gy')), may hold values from -1 to 4095, as said below
- decode_senders: int32 [3, 16384], P(None, ('gx', 'gy')), may hold values from 0 to 4095, as said below
- encoder_edges: bfloat16 [3, 512, 512], replicated, may hold values from -0.25 to 0.25
- encoder_edgebias: float32 [2, 512], replicated, may hold values from -3 to 3
- encoder_nodes: bfloat16 [3, 512, 512], replicated, may hold values from -0.25 to 0.25
- encoder_nodebias: float32 [2, 512], replicated, may hold values from -3 to 3
- process_edges: bfloat16 [3, 512, 512], replicated, may hold values from -0.25 to 0.25
- process_edgebias: float32 [2, 512], replicated, may hold values from -3 to 3
- process_nodes: bfloat16 [3, 512, 512], replicated, may hold values from -0.25 to 0.25
- process_nodebias: float32 [2, 512], replicated, may hold values from -3 to 3
- decoder_edges: bfloat16 [3, 512, 512], replicated, may hold values from -0.25 to 0.25
- decoder_edgebias: float32 [2, 512], replicated, may hold values from -3 to 3
- decoder_nodes: bfloat16 [3, 512, 512], replicated, may hold values from -0.25 to 0.25
- decoder_nodebias: float32 [2, 512], replicated, may hold values from -3 to 3
Outputs:
- decoded_grid: bfloat16 [16384, 512], P(('gx', 'gy'))
- processed_mesh: bfloat16 [4096, 512], P(('gx', 'gy'))
The draws below stay inside these ranges and needn't reach their ends.
Inputs may be any that keep to these rules, and one draw needn't show every extreme that they name: `encode_senders`: devices form a torus of regions, device number = gx index * gy size + gy index, and device d owns grid points d * 512 to (d + 1) * 512 - 1. In each column the live senders come first, then -1; a column has 8 to 32 live senders and some column has 32. A live sender is a grid point of the column's own device, or one of the first 128 grid points of one of the eight devices around it on the torus (wrapping on both axes). `mesh_senders`: device d owns mesh nodes d * 128 to (d + 1) * 128 - 1. In each column the live senders come first, then -1; a column has 8 to 32 live senders and some column has 32. A live sender is a mesh node of the column's own device, or one of the first 32 mesh nodes of one of the eight devices around it on the torus, or one of the first 4 mesh nodes of any device. `decode_senders`: every entry is live: a mesh node of the grid point's own device, or one of the first 32 mesh nodes of one of the eight devices around it on the torus.
All inputs are finite; a program needn't handle non-finite values.
Results may differ from the reference program's by a relative error of at most 0.013.
Values may be sent and summed in bfloat16 or wider, within the bound.
No kernel may reach another device: no remote copies, remote signals or barrier semaphores. Data moves between devices by JAX's collectives and lax.ppermute only.
A program may use at most 64 MiB of HBM per device.

```python
import jax
import jax.numpy as jnp
from jax import lax

D = 512
G_DEV = 512
M_DEV = 128
K1 = 32
KM = 32
K3 = 3
CM = 4
GRID = 16384
MESH = 4096
N_GX = 4
N_GY = 8


def sender_table(key, degree, receivers, senders, border, coarse, own_share, far_share, least):
    devices = N_GX * N_GY
    total = receivers * devices
    keys = jax.random.split(key, 7)
    column = jnp.arange(total, dtype=jnp.int32)
    device = column // receivers
    place_x = device // N_GY
    place_y = device % N_GY
    kind = jax.random.randint(keys[0], (degree, total), 0, 100)
    which = jax.random.randint(keys[1], (degree, total), 0, 8)
    table_x = jnp.array([-1, -1, -1, 0, 0, 1, 1, 1], jnp.int32)
    table_y = jnp.array([-1, 0, 1, -1, 1, -1, 0, 1], jnp.int32)
    near_x = (place_x[None] + table_x[which]) % N_GX
    near_y = (place_y[None] + table_y[which]) % N_GY
    near_device = near_x * N_GY + near_y
    far_device = jax.random.randint(keys[2], (degree, total), 0, devices)
    own_row = jax.random.randint(keys[3], (degree, total), 0, senders)
    near_row = jax.random.randint(keys[4], (degree, total), 0, border)
    far_row = jax.random.randint(keys[5], (degree, total), 0, max(coarse, 1))
    is_own = kind < own_share
    is_far = kind >= 100 - far_share
    source = jnp.where(is_own, device[None], jnp.where(is_far, far_device, near_device))
    offset = jnp.where(is_own, own_row, jnp.where(is_far, far_row, near_row))
    sender_ids = (source * senders + offset).astype(jnp.int32)
    polar = (place_x == 0) | (place_x == N_GX - 1)
    split = least + (degree - least) * 3 // 4
    lower = jnp.where(polar, split, least)
    upper = jnp.where(polar, degree + 1, split + 1)
    counts = jax.random.randint(keys[6], (total,), lower, upper)
    leading = column % receivers == 0
    counts = jnp.where(leading & polar, degree, counts)
    slots = jnp.arange(degree, dtype=jnp.int32)[:, None]
    return jnp.where(slots < counts[None], sender_ids, -1).astype(jnp.int32)


def draw_encode_senders(key, part):
    return sender_table(jax.random.fold_in(key, 11), K1, M_DEV, G_DEV, G_DEV // 4, 0, 50, 0, K1 // 4)


def draw_mesh_senders(key, part):
    return sender_table(jax.random.fold_in(key, 23), KM, M_DEV, M_DEV, M_DEV // 4, CM, 40, 30, KM // 4)


def draw_decode_senders(key, part):
    return sender_table(jax.random.fold_in(key, 37), K3, G_DEV, M_DEV, M_DEV // 4, 0, 50, 0, K3)


def block_scale(own_key, extent, cuts, low, high):
    factor_of = 1.0
    for dim, blocks in cuts:
        draws = jax.random.uniform(jax.random.fold_in(jax.random.fold_in(own_key, 6), dim), (blocks,), jnp.float32, low / len(cuts), high / len(cuts))
        factor_of = factor_of * jnp.repeat(jnp.exp(draws), extent[dim] // blocks).reshape((-1,) + (1,) * (len(extent) - 1 - dim))
    return factor_of


def noise(key, shape, scale, limit, shards=(), kind=jnp.bfloat16):
    result = jax.random.normal(key, shape, jnp.float32) * scale
    if len(shards) > 0:
        result = block_scale(key, shape, shards, -0.22, 0.18) * result
    return jnp.clip(result, min=-limit, max=limit).astype(kind)


def setup_inputs(seed: int = 0) -> dict:
    arg_keys = jax.random.split(jax.random.key(seed), 18)
    return {
        "grid_latent": noise(arg_keys[0], (GRID, D), 1.0, 6.0, ((0, 32),)),
        "mesh_latent": noise(arg_keys[1], (MESH, D), 1.0, 6.0, ((0, 32),)),
        "encode_senders": draw_encode_senders(jax.random.fold_in(arg_keys[17], 71), 0),
        "mesh_senders": draw_mesh_senders(jax.random.fold_in(arg_keys[17], 71), 0),
        "decode_senders": draw_decode_senders(jax.random.fold_in(arg_keys[17], 71), 0),
        "encoder_edges": noise(arg_keys[5], (3, D, D), D ** -0.5, 0.25),
        "encoder_edgebias": noise(arg_keys[6], (2, D), 0.3, 3.0, (), jnp.float32),
        "encoder_nodes": noise(arg_keys[7], (3, D, D), D ** -0.5, 0.25),
        "encoder_nodebias": noise(arg_keys[8], (2, D), 0.3, 3.0, (), jnp.float32),
        "process_edges": noise(arg_keys[9], (3, D, D), D ** -0.5, 0.25),
        "process_edgebias": noise(arg_keys[10], (2, D), 0.3, 3.0, (), jnp.float32),
        "process_nodes": noise(arg_keys[11], (3, D, D), D ** -0.5, 0.25),
        "process_nodebias": noise(arg_keys[12], (2, D), 0.3, 3.0, (), jnp.float32),
        "decoder_edges": noise(arg_keys[13], (3, D, D), D ** -0.5, 0.25),
        "decoder_edgebias": noise(arg_keys[14], (2, D), 0.3, 3.0, (), jnp.float32),
        "decoder_nodes": noise(arg_keys[15], (3, D, D), D ** -0.5, 0.25),
        "decoder_nodebias": noise(arg_keys[16], (2, D), 0.3, 3.0, (), jnp.float32),
    }


def project(latent, weight):
    return jnp.dot(latent, weight, preferred_element_type=jnp.float32)

def finish(preact, weights, vectors):
    hidden = jax.nn.silu(preact).astype(jnp.bfloat16)
    output = jnp.dot(hidden, weights[2], preferred_element_type=jnp.float32)
    centre = lax.optimization_barrier(jnp.mean(output, axis=-1, keepdims=True))
    centred = output - centre
    spread = lax.optimization_barrier(jnp.mean(centred * centred, axis=-1, keepdims=True))
    return centred * lax.rsqrt(spread + 1e-05) * (1.0 + vectors[1])

def block_size(count, degree):
    target = max(1, 4096 // degree)
    chosen = min(count, target)
    while count % chosen:
        chosen -= 1
    return chosen

def aggregate(table, receiving, positions, active, weights, vectors):
    degree, count = positions.shape
    chosen = block_size(count, degree)
    blocks = count // chosen
    width = table.shape[1]
    shifted = (receiving + vectors[0]).reshape(blocks, chosen, width)
    places = positions.reshape(degree, blocks, chosen).transpose(1, 0, 2)
    masks = active.reshape(degree, blocks, chosen).transpose(1, 0, 2)

    def one_block(item):
        base, place, present = item
        gathered = jnp.take(table, place, axis=0)
        preact = gathered + base[None]
        message = finish(preact.reshape(degree * chosen, width), weights, vectors)
        message = message.reshape(degree, chosen, width)
        return lax.optimization_barrier(jnp.sum(jnp.where(present[..., None], message, 0.0), axis=0))
    return lax.map(one_block, (shifted, places, masks)).reshape(count, width)

def update(latent, summed, weights, vectors):
    preact = project(latent, weights[0]) + project(summed.astype(jnp.bfloat16), weights[1]) + vectors[0]
    return (latent.astype(jnp.float32) + finish(preact, weights, vectors)).astype(jnp.bfloat16)

def edge_sums(sender_latent, receiver_latent, senders, weights, vectors):
    table = project(sender_latent, weights[0])
    receiving = project(receiver_latent, weights[1])
    return aggregate(table, receiving, jnp.maximum(senders, 0).astype(jnp.int32), senders >= 0, weights, vectors)

def reference(grid_latent, mesh_latent, encode_senders, mesh_senders, decode_senders, encoder_edges, encoder_edgebias, encoder_nodes, encoder_nodebias, process_edges, process_edgebias, process_nodes, process_nodebias, decoder_edges, decoder_edgebias, decoder_nodes, decoder_nodebias):
    summed = edge_sums(grid_latent, mesh_latent, encode_senders, encoder_edges, encoder_edgebias)
    encoded = update(mesh_latent, summed, encoder_nodes, encoder_nodebias)
    summed = edge_sums(encoded, encoded, mesh_senders, process_edges, process_edgebias)
    processed = update(encoded, summed, process_nodes, process_nodebias)
    summed = edge_sums(processed, grid_latent, decode_senders, decoder_edges, decoder_edgebias)
    decoded = update(grid_latent, summed, decoder_nodes, decoder_nodebias)
    return (decoded, processed)
```

```python
import functools

import jax
import jax.numpy as jnp
from jax import lax
from jax.experimental import pallas as pl
from jax.experimental.pallas import tpu as pltpu
from jax.sharding import PartitionSpec as P

AXES = ("gx", "gy")
CM = 4
EPS = 1e-05
BF = jnp.bfloat16
F32 = jnp.float32
I32 = jnp.int32
SDS = jax.ShapeDtypeStruct


def mm(a, b):
    return jnp.dot(a, b, preferred_element_type=F32)


def half_silu(half):
    return (half + half * jnp.tanh(half)).astype(BF)


def inverse_norm(centred):
    spread = jnp.mean(centred * centred, axis=-1, keepdims=True)
    return lax.rsqrt(spread + EPS)


def centre(w):
    w = w.astype(F32)
    return (w - jnp.mean(w, axis=-1, keepdims=True)).astype(BF)


class Mover:
    def __init__(self, sems):
        self.sems = sems
        self.used = 0

    def start(self, source, target):
        copy = pltpu.make_async_copy(source, target, self.sems.at[self.used])
        self.used += 1
        copy.start()
        return copy


def launch(body, name, ins, outs, scratch, copies, flops, nbytes):
    hbm = pl.BlockSpec(memory_space=pltpu.HBM)
    return pl.pallas_call(
        body,
        out_shape=outs,
        in_specs=[hbm] * len(ins),
        out_specs=[hbm] * len(outs),
        scratch_shapes=[pltpu.VMEM(s, d) for s, d in scratch] + [pltpu.SemaphoreType.DMA((copies,))],
        compiler_params=pltpu.CompilerParams(vmem_limit_bytes=56 << 20),
        cost_estimate=pl.CostEstimate(flops=flops, bytes_accessed=nbytes, transcendentals=0),
        name=name,
    )(*ins)


def border_kernel(x, w, out, x_v, w_v, out_v, sems):
    mover = Mover(sems)
    loads = [mover.start(x.at[pl.ds(0, x_v.shape[0])], x_v), mover.start(w.at[0], w_v)]
    for load in loads:
        load.wait()
    out_v[...] = (mm(x_v[...], w_v[...]) * 0.5).astype(BF)
    mover.start(out_v, out).wait()


def split(value, by):
    if by & (by - 1) == 0:
        return value >> (by.bit_length() - 1), value & (by - 1)
    return value // by, value % by


def locate(ids, rows, border, coarse, sizes, places):
    size_x, size_y = sizes
    place_x, place_y = places
    owner, offset = split(jnp.maximum(ids, 0), rows)
    owner_x, owner_y = split(owner, size_y)
    step_x = owner_x - place_x
    step_x = jnp.where(step_x < 0, step_x + size_x, step_x)
    step_y = owner_y - place_y
    step_y = jnp.where(step_y < 0, step_y + size_y, step_y)
    ahead_x, ahead_y = (place_x & 1) == 0, (place_y & 1) == 0
    pair_x = jnp.where(ahead_x, 1, size_x - 1)
    pair_y = jnp.where(ahead_y, 1, size_y - 1)
    kind_x = jnp.where(step_x == 0, 0, jnp.where(step_x == pair_x, 1, 2))
    kind_y = jnp.where(step_y == 0, 0, jnp.where(step_y == pair_y, 1, 2))
    near_x = (step_x <= 1) | (step_x == size_x - 1)
    near_y = (step_y <= 1) | (step_y == size_y - 1)
    group = 3 * border + coarse * size_y
    first = jnp.where(kind_x == 0, rows - border, rows + 2 * border + (kind_x - 1) * group)
    found = first + kind_y * border + offset
    if coarse:
        flip = owner_y ^ place_y
        column = jnp.where(kind_x == 0, 0, 3 * border)
        far = first + column
        tail = rows + 2 * border + 2 * group
        far = jnp.where(kind_x == 0, tail, far)
        far = jnp.where(near_x, far, tail + (step_x - 1) * coarse * size_y)
        far = far + (flip ^ (flip >> 1)) * coarse + offset
        nearby = near_x & near_y & (offset < border)
        found = jnp.where(nearby, found, far)
    found = jnp.where((step_x == 0) & (step_y == 0), offset, found)
    return jnp.where(ids >= 0, found, -1)


def turned(found):
    degree, count = found.shape
    pad = -degree % 8
    if pad:
        found = jnp.concatenate([found, jnp.full((pad, count), -1, I32)], axis=0)
    return found.astype(F32).T.astype(I32)


def prepare_kernel(
    sizes, shapes,
    grid, mesh, eids, mids, dids, ee, en, pe, pn, de, dn, eb, db,
    own_o, ebase_o, dbase_o, eat_o, mat_o, dat_o, ee2_o, en2_o, pe2_o, pn2_o, de2_o, dn2_o,
    grid_v, mesh_v, eids_v, mids_v, dids_v, w0_v, w1_v, wd_v, eb_v, db_v, w2_v,
    own_v, ebase_v, dbase_v, eat_v, mat_v, dat_v, c2_v, sems,
):
    mover = Mover(sems)
    grid_rows, mesh_rows, grid_border, mesh_border = shapes
    heads = [
        mover.start(a, b)
        for a, b in (
            (eids, eids_v), (mids, mids_v), (dids, dids_v), (grid, grid_v), (mesh, mesh_v),
            (ee.at[0], w0_v), (ee.at[1], w1_v), (de.at[1], wd_v), (eb, eb_v), (db, db_v),
        )
    ]
    seconds = [mover.start(w.at[2], w2_v.at[i]) for i, w in enumerate((ee, en, pe, pn, de, dn))]
    for head in heads:
        head.wait()
    places = (lax.axis_index("gx"), lax.axis_index("gy"))
    tails = []
    own_v[...] = (mm(grid_v[...], w0_v[...]) * 0.5).astype(BF)
    tails.append(mover.start(own_v, own_o))
    eat_v[...] = turned(locate(eids_v[...], grid_rows, grid_border, 0, sizes, places))
    tails.append(mover.start(eat_v, eat_o))
    ebase_v[...] = (mm(mesh_v[...], w1_v[...]) + eb_v[0:1, :]) * 0.5
    tails.append(mover.start(ebase_v, ebase_o))
    for i, (second, out) in enumerate(zip(seconds, (ee2_o, en2_o, pe2_o, pn2_o, de2_o, dn2_o))):
        second.wait()
        c2_v[i] = centre(w2_v[i])
        tails.append(mover.start(c2_v.at[i], out))
    mat_v[...] = turned(locate(mids_v[...], mesh_rows, mesh_border, CM, sizes, places))
    tails.append(mover.start(mat_v, mat_o))
    dat_v[...] = turned(locate(dids_v[...], mesh_rows, mesh_border, 0, sizes, places))
    tails.append(mover.start(dat_v, dat_o))
    dbase_v[...] = (mm(grid_v[...], wd_v[...]) + db_v[0:1, :]) * 0.5
    tails.append(mover.start(dbase_v, dbase_o))
    for tail in tails:
        tail.wait()


def edge_sum(places, degree, table, base, w2, vectors, slots_per_step):
    rows, width = base.shape
    lanes = lax.broadcasted_iota(I32, (rows, table.shape[0]), 1)
    total = jnp.zeros((rows, width), F32)
    for first in range(0, degree, slots_per_step):
        ks = range(first, min(first + slots_per_step, degree))
        count = len(ks)
        selector = jnp.concatenate(
            [(places[:, k : k + 1] == lanes).astype(F32).astype(BF) for k in ks], axis=0
        )
        half = mm(selector, table[...]).reshape(count, rows, width) + base[None]
        hidden = half_silu(half.reshape(count * rows, width))
        y = mm(hidden, w2)
        scale = inverse_norm(y).reshape(count, rows, 1)
        y = y.reshape(count, rows, width)
        for i, k in enumerate(ks):
            live = (places[:, k : k + 1] >= 0).astype(F32)
            total = total + y[i] * (scale[i] * live)
    return total * (1.0 + vectors[1:2, :])


def node_update(x, summed, w0, w1, w2, vectors):
    half = (mm(x, w0) + mm(summed.astype(BF), w1) + vectors[0:1, :]) * 0.5
    y = mm(half_silu(half), w2)
    return (x.astype(F32) + y * inverse_norm(y) * (1.0 + vectors[1:2, :])).astype(BF)


def mesh_stage(x, x_at, places, at, count, pieces, base, base_at, ew2, ev, nw, nw2, nv, following, fv, joined, steps, name):
    width = x.shape[1]
    degree = places.shape[1]
    table_rows = sum(p.shape[0] for p in pieces)
    again = fv is not None
    ins = [x, places, base, ew2, ev, nw, nw2, nv, following] + ([fv] if again else []) + ([joined] if joined is not None else []) + pieces
    rows_out = count + (joined.shape[0] if joined is not None else 0)
    outs = [SDS((rows_out, width), BF), SDS((count, width), BF)] + ([SDS((count, width), F32)] if again else [])
    scratch = [
        ((count, width), BF), ((count, degree), I32), ((count, width), F32), ((width, width), BF), ((2, width), F32),
        ((2, width, width), BF), ((width, width), BF), ((2, width), F32), ((2, width, width), BF), ((2, width), F32),
        ((table_rows, width), BF), ((rows_out, width), BF), ((count, width), BF), ((count, width), F32),
    ]

    def body(*refs):
        refs = list(refs)
        x_h, places_h, base_h, ew2_h, ev_h, nw_h, nw2_h, nv_h, follow_h = refs[:9]
        refs = refs[9:]
        fv_h = refs.pop(0) if again else None
        joined_h = refs.pop(0) if joined is not None else None
        pieces_h, refs = refs[: len(pieces)], refs[len(pieces) :]
        outs_h, refs = refs[: len(outs)], refs[len(outs) :]
        (x_v, places_v, base_v, ew2_v, ev_v, nw_v, nw2_v, nv_v, follow_v, fv_v, table_v, new_v, proj_v, nbase_v, sems) = refs
        mover = Mover(sems)
        early = []
        start = 0
        for piece in pieces_h:
            early.append(mover.start(piece, table_v.at[pl.ds(start, piece.shape[0])]))
            start += piece.shape[0]
        early.append(mover.start(places_h.at[pl.ds(at, count)], places_v))
        early.append(mover.start(base_h.at[pl.ds(base_at, count)], base_v))
        early.append(mover.start(ew2_h, ew2_v))
        early.append(mover.start(ev_h, ev_v))
        late = [
            mover.start(x_h.at[pl.ds(x_at, count)], x_v),
            mover.start(nw_h.at[pl.ds(0, 2)], nw_v),
            mover.start(nw2_h, nw2_v),
            mover.start(nv_h, nv_v),
            mover.start(follow_h.at[pl.ds(0, 2)], follow_v),
        ]
        if again:
            late.append(mover.start(fv_h, fv_v))
        if joined is not None:
            late.append(mover.start(joined_h, new_v.at[pl.ds(0, joined.shape[0])]))
        for load in early:
            load.wait()
        summed = edge_sum(places_v[...], degree, table_v, base_v[...], ew2_v[...], ev_v, steps)
        for load in late:
            load.wait()
        new = node_update(x_v[...], summed, nw_v[0], nw_v[1], nw2_v[...], nv_v)
        new_v[pl.ds(rows_out - count, count), :] = new
        proj_v[...] = (mm(new, follow_v[0]) * 0.5).astype(BF)
        tails = [mover.start(proj_v, outs_h[1]), mover.start(new_v, outs_h[0])]
        if again:
            nbase_v[...] = (mm(new, follow_v[1]) + fv_v[0:1, :]) * 0.5
            tails.append(mover.start(nbase_v, outs_h[2]))
        for tail in tails:
            tail.wait()

    flops = count * degree * (2 * width * table_rows + 2 * width * width)
    return launch(body, name, ins, outs, scratch, len(pieces) + 16, flops, 6 << 20)


def decode_stage(x, places, degree, pieces, base, ew2, ev, nw, nw2, nv, block):
    rows, width = x.shape
    table_rows = sum(p.shape[0] for p in pieces)
    ins = [x, places, base, ew2, ev, nw, nw2, nv] + pieces
    outs = [SDS((rows, width), BF)]
    scratch = [
        ((rows, width), BF), (places.shape, I32), ((rows, width), F32), ((width, width), BF), ((2, width), F32),
        ((2, width, width), BF), ((width, width), BF), ((2, width), F32), ((table_rows, width), BF), ((rows, width), BF),
    ]

    def body(*refs):
        refs = list(refs)
        x_h, places_h, base_h, ew2_h, ev_h, nw_h, nw2_h, nv_h = refs[:8]
        pieces_h = refs[8 : 8 + len(pieces)]
        out_h, x_v, places_v, base_v, ew2_v, ev_v, nw_v, nw2_v, nv_v, table_v, new_v, sems = refs[8 + len(pieces) :]
        mover = Mover(sems)
        loads = []
        start = 0
        for piece in pieces_h:
            loads.append(mover.start(piece, table_v.at[pl.ds(start, piece.shape[0])]))
            start += piece.shape[0]
        loads += [
            mover.start(a, b)
            for a, b in (
                (places_h, places_v), (base_h, base_v), (ew2_h, ew2_v), (ev_h, ev_v), (x_h, x_v),
                (nw_h.at[pl.ds(0, 2)], nw_v), (nw2_h, nw2_v), (nv_h, nv_v),
            )
        ]
        for load in loads:
            load.wait()
        tails = []
        for at in range(0, rows, block):
            part = pl.ds(at, block)
            summed = edge_sum(places_v[part, :], degree, table_v, base_v[part, :], ew2_v[...], ev_v, degree)
            new_v[part, :] = node_update(x_v[part, :], summed, nw_v[0], nw_v[1], nw2_v[...], nv_v)
            tails.append(mover.start(new_v.at[part], out_h.at[part]))
        for tail in tails:
            tail.wait()

    flops = rows * degree * (2 * width * table_rows + 2 * width * width)
    return launch(body, "decode", ins, outs, scratch, len(pieces) + 8 + rows // block, flops, 6 << 20)[0]


def sender(size_x, size_y):
    def send(rows, move):
        pairs = []
        for i in range(size_x):
            for j in range(size_y):
                a, b = move(i, j)
                pairs.append((i * size_y + j, (a % size_x) * size_y + b % size_y))
        return lax.ppermute(rows, AXES, pairs)

    return send


def next_pair(i):
    return i + 1 if i % 2 else i - 1


def per_device(
    grid_latent, mesh_latent, encode_senders, mesh_senders, decode_senders,
    encoder_edges, encoder_edgebias, encoder_nodes, encoder_nodebias,
    process_edges, process_edgebias, process_nodes, process_nodebias,
    decoder_edges, decoder_edgebias, decoder_nodes, decoder_nodebias,
):
    grid_rows, width = grid_latent.shape
    mesh_rows = mesh_latent.shape[0]
    grid_border = grid_rows // 4
    mesh_border = mesh_rows // 4
    size_x = lax.axis_size("gx")
    size_y = lax.axis_size("gy")
    square = 2 * width * width
    send = sender(size_x, size_y)
    pair_x = lambda i, j: (i ^ 1, j)
    next_x = lambda i, j: (next_pair(i), j)
    pair_y = lambda i, j: (i, j ^ 1)
    next_y = lambda i, j: (i, next_pair(j))

    border = launch(
        border_kernel, "project_border", [grid_latent, encoder_edges], [SDS((grid_border, width), BF)],
        [((grid_border, width), BF), ((width, width), BF), ((grid_border, width), BF)], 3, grid_border * square, 1 << 20,
    )[0]
    e = send(border, pair_x)
    o = send(border, next_x)
    z = send(border, next_y)
    c = send(border, pair_y)

    degrees = [ids.shape[0] + -ids.shape[0] % 8 for ids in (encode_senders, mesh_senders, decode_senders)]
    square_shape = ((width, width), BF)
    outs = [
        ((grid_rows, width), BF), ((mesh_rows, width), F32), ((grid_rows, width), F32),
        ((mesh_rows, degrees[0]), I32), ((mesh_rows, degrees[1]), I32), ((grid_rows, degrees[2]), I32),
    ]
    own, base, grid_base, encode_at, mesh_at, decode_at, ee2, en2, pe2, pn2, de2, dn2 = launch(
        functools.partial(prepare_kernel, (size_x, size_y), (grid_rows, mesh_rows, grid_border, mesh_border)), "prepare",
        [
            grid_latent, mesh_latent, encode_senders, mesh_senders, decode_senders, encoder_edges, encoder_nodes,
            process_edges, process_nodes, decoder_edges, decoder_nodes, encoder_edgebias, decoder_edgebias,
        ],
        [SDS(s, d) for s, d in outs + [square_shape] * 6],
        [
            ((grid_rows, width), BF), ((mesh_rows, width), BF), (encode_senders.shape, I32), (mesh_senders.shape, I32),
            (decode_senders.shape, I32), square_shape, square_shape, square_shape, ((2, width), F32), ((2, width), F32),
            ((6, width, width), BF), *outs, ((6, width, width), BF),
        ],
        28, 2 * grid_rows * square, 12 << 20,
    )
    ec = send(e, pair_y)
    oc = send(o, pair_y)
    ez = send(z, pair_x)
    oz = send(z, next_x)
    pieces = [own, c, z, e, ec, ez, o, oc, oz]

    cuts = [0, mesh_border, mesh_border * 5 // 2, mesh_rows]
    encoded = []
    for at, end in zip(cuts, cuts[1:]):
        encoded.append(
            mesh_stage(
                mesh_latent, at, encode_at, at, end - at, pieces, base, at, ee2, encoder_edgebias, encoder_nodes, en2,
                encoder_nodebias, process_edges, process_edgebias, None, 512 // (end - at), "encode",
            )
        )

    border = encoded[0][1]
    c = send(border, pair_y)
    z = send(border, next_y)
    column = jnp.concatenate([border[:CM], c[:CM]], axis=0)
    step = 2
    while step < size_y:
        flip = 2 * step - 1
        column = jnp.concatenate([column, send(column, lambda i, j, flip=flip: (i, j ^ flip))], axis=0)
        step *= 2
    stack = jnp.concatenate([border, c, z, column], axis=0)
    e = send(stack, pair_x)
    o = send(stack, next_x)
    far = [send(column, lambda i, j, d=d: (i - d, j)) for d in range(2, size_x - 1)]
    pieces = [part[1] for part in encoded] + [c, z, e, o, column] + far

    x = jnp.concatenate([part[0] for part in encoded[1:]], axis=0)
    base = jnp.concatenate([part[2] for part in encoded[1:]], axis=0)
    first = mesh_stage(
        encoded[0][0], 0, mesh_at, 0, mesh_border, pieces, encoded[0][2], 0, pe2, process_edgebias, process_nodes, pn2,
        process_nodebias, decoder_edges, None, None, 512 // mesh_border, "process",
    )
    border = first[1]
    c = send(border, pair_y)
    z = send(border, next_y)
    rest = mesh_rows - mesh_border
    processed, projected = mesh_stage(
        x, 0, mesh_at, mesh_border, rest, pieces, base, 0, pe2, process_edgebias, process_nodes, pn2,
        process_nodebias, decoder_edges, None, first[0], 4, "process",
    )
    stack = jnp.concatenate([border, c, z], axis=0)
    e = send(stack, pair_x)
    o = send(stack, next_x)
    decoded = decode_stage(
        grid_latent, decode_at, decode_senders.shape[0], [border, projected, c, z, e, o], grid_base, de2, decoder_edgebias,
        decoder_nodes, dn2, decoder_nodebias, 128,
    )
    return (decoded, processed)


def solution(mesh):
    rows = P(AXES, None)
    senders = P(None, AXES)
    return jax.shard_map(
        per_device,
        mesh=mesh,
        in_specs=(rows, rows, senders, senders, senders) + (P(),) * 12,
        out_specs=(rows, rows),
        check_vma=False,
    )
```

```python
import functools

import jax
import jax.numpy as jnp
from jax import lax
from jax.experimental import pallas as pl
from jax.experimental.pallas import tpu as pltpu
from jax.sharding import PartitionSpec as P

AXES = ("gx", "gy")
CM = 4
EPS = 1e-05
BF = jnp.bfloat16
F32 = jnp.float32
I32 = jnp.int32
SDS = jax.ShapeDtypeStruct


def mm(a, b):
    return jnp.dot(a, b, preferred_element_type=F32)


def half_silu(half):
    return (half + half * jnp.tanh(half)).astype(BF)


def inverse_norm(centred):
    spread = jnp.mean(centred * centred, axis=-1, keepdims=True)
    return lax.rsqrt(spread + EPS)


def centre(w):
    w = w.astype(F32)
    return (w - jnp.mean(w, axis=-1, keepdims=True)).astype(BF)


class Mover:
    def __init__(self, sems):
        self.sems = sems
        self.used = 0

    def start(self, source, target):
        copy = pltpu.make_async_copy(source, target, self.sems.at[self.used])
        self.used += 1
        copy.start()
        return copy


def launch(body, name, ins, outs, scratch, copies, flops, nbytes, far_ins=(), far_outs=(), mib=10):
    near = pl.BlockSpec(memory_space=pltpu.VMEM)
    far = pl.BlockSpec(memory_space=pltpu.HBM)
    sems = [pltpu.SemaphoreType.DMA((copies,))] if copies else []
    ins = [pltpu.with_memory_space_constraint(x, pltpu.HBM) if i in far_ins else x for i, x in enumerate(ins)]
    return pl.pallas_call(
        body,
        out_shape=outs,
        in_specs=[far if i in far_ins else near for i in range(len(ins))],
        out_specs=[far if i in far_outs else near for i in range(len(outs))],
        scratch_shapes=[pltpu.VMEM(s, d) for s, d in scratch] + sems,
        compiler_params=pltpu.CompilerParams(vmem_limit_bytes=mib << 20),
        cost_estimate=pl.CostEstimate(flops=flops, bytes_accessed=nbytes, transcendentals=0),
        name=name,
    )(*ins)


def glue(*parts):
    width = parts[0][0].shape[1]
    total = sum(rows for _, rows in parts)

    def body(*refs):
        out = refs[-1]
        if any(rows % 16 for _, rows in parts):
            values = [ref[pl.ds(0, rows), :].astype(F32) for ref, (_, rows) in zip(refs, parts)]
            out[...] = jnp.concatenate(values, axis=0).astype(BF)
        else:
            start = 0
            for ref, (_, rows) in zip(refs, parts):
                out[pl.ds(start, rows), :] = ref[pl.ds(0, rows), :]
                start += rows

    return launch(body, "glue", [x for x, _ in parts], [SDS((total, width), BF)], [], 0, 1 << 10, 1 << 18, mib=2)[0]


def border_kernel(x, w, out, x_v, w_v, sems):
    mover = Mover(sems)
    quarter = w_v.shape[0] // 4
    loads = [mover.start(x.at[pl.ds(0, x_v.shape[0])], x_v)]
    for i in range(4):
        part = pl.ds(i * quarter, quarter)
        loads.append(mover.start(w.at[0, part], w_v.at[part]))
    for load in loads:
        load.wait()
    out[...] = (mm(x_v[...], w_v[...]) * 0.5).astype(BF)


def split(value, by):
    if by & (by - 1) == 0:
        return value >> (by.bit_length() - 1), value & (by - 1)
    return value // by, value % by


def locate(ids, rows, border, coarse, sizes, places, early=False):
    size_x, size_y = sizes
    place_x, place_y = places
    owner, offset = split(jnp.maximum(ids, 0), rows)
    owner_x, owner_y = split(owner, size_y)
    step_x = owner_x - place_x
    step_x = jnp.where(step_x < 0, step_x + size_x, step_x)
    step_y = owner_y - place_y
    step_y = jnp.where(step_y < 0, step_y + size_y, step_y)
    ahead_x, ahead_y = (place_x & 1) == 0, (place_y & 1) == 0
    pair_x = jnp.where(ahead_x, 1, size_x - 1)
    pair_y = jnp.where(ahead_y, 1, size_y - 1)
    kind_x = jnp.where(step_x == 0, 0, jnp.where(step_x == pair_x, 1, 2))
    kind_y = jnp.where(step_y == 0, 0, jnp.where(step_y == pair_y, 1, 2))
    near_x = (step_x <= 1) | (step_x == size_x - 1)
    near_y = (step_y <= 1) | (step_y == size_y - 1)
    group = 3 * border + coarse * size_y
    first = jnp.where(kind_x == 0, rows - border, rows + 2 * border + (kind_x - 1) * group)
    found = first + kind_y * border + offset
    if early:
        slot = jnp.where(kind_x == 0, kind_y - 1, jnp.where(kind_y == 0, kind_x + 1, 2 * kind_x + kind_y + 1))
        found = rows + slot * border + offset
    if coarse:
        flip = owner_y ^ place_y
        column = jnp.where(kind_x == 0, 0, 3 * border)
        far = first + column
        tail = rows + 2 * border + 2 * group
        far = jnp.where(kind_x == 0, tail, far)
        far = jnp.where(near_x, far, tail + (step_x - 1) * coarse * size_y)
        far = far + (flip ^ (flip >> 1)) * coarse + offset
        nearby = near_x & near_y & (offset < border)
        found = jnp.where(nearby, found, far)
    found = jnp.where((step_x == 0) & (step_y == 0), offset, found)
    return jnp.where(ids >= 0, found, -1)


def turned(found):
    degree, count = found.shape
    pad = -degree % 8
    if pad:
        found = jnp.concatenate([found, jnp.full((pad, count), -1, I32)], axis=0)
    return found.astype(F32).T.astype(I32)


def prepare_kernel(
    sizes, shapes,
    grid, mesh, eids, mids, dids, ee, en, pe, pn, de, dn, eb, db,
    grid_o, mesh_o, own, ebase, dbase, eat, mat, dat, ee2, en2, pe2, pn2, de2, dn2, en01, pe01, pn01, de01, dn01,
    eids_v, mids_v, dids_v, w0_v, w1_v, eb_v, db_v, w2_v, sems,
):
    mover = Mover(sems)
    grid_rows, mesh_rows, grid_border, mesh_border = shapes
    heads = [
        mover.start(a, b)
        for a, b in (
            (eids, eids_v), (mids, mids_v), (dids, dids_v), (grid, grid_o), (mesh, mesh_o),
            (ee.at[0], w0_v), (ee.at[1], w1_v), (eb, eb_v), (db, db_v),
        )
    ]
    seconds = [mover.start(w.at[2], w2_v.at[i]) for i, w in enumerate((ee, en, pe, pn, de, dn))]
    pairs = [
        mover.start(w.at[pl.ds(0, 2)], out)
        for w, out in ((en, en01), (pe, pe01), (de, de01), (pn, pn01), (dn, dn01))
    ]
    for head in heads:
        head.wait()
    places = (lax.axis_index("gx"), lax.axis_index("gy"))
    eat[...] = turned(locate(eids_v[...], grid_rows, grid_border, 0, sizes, places, True))
    own[...] = (mm(grid_o[...], w0_v[...]) * 0.5).astype(BF)
    ebase[...] = (mm(mesh_o[...], w1_v[...]) + eb_v[0:1, :]) * 0.5
    mat[...] = turned(locate(mids_v[...], mesh_rows, mesh_border, CM, sizes, places))
    dat[...] = turned(locate(dids_v[...], mesh_rows, mesh_border, 0, sizes, places))
    for i, (second, out) in enumerate(zip(seconds, (ee2, en2, pe2, pn2, de2, dn2))):
        second.wait()
        out[...] = centre(w2_v[i])
    for pair in pairs:
        pair.wait()
    dbase[...] = (mm(grid_o[...], de01[1]) + db_v[0:1, :]) * 0.5


def chosen(places, ks, lanes):
    return jnp.concatenate([(places[:, k : k + 1] == lanes).astype(F32).astype(BF) for k in ks], axis=0)


def edge_sum(places, degree, table, base, w2, vectors, slots, lift=0, begun=None):
    rows, width = base.shape
    lanes = lift + lax.broadcasted_iota(I32, (rows, table.shape[0]), 1)
    groups = [range(k, min(k + slots, degree)) for k in range(0, degree, slots)]

    def gather(ks):
        half = mm(chosen(places, ks, lanes), table[...])
        if begun is not None:
            ref, start = begun
            half = half + ref[pl.ds(start + ks[0] * rows, len(ks) * rows), :].astype(F32)
        return half.reshape(len(ks), rows, width) + base[None]

    total = jnp.zeros((rows, width), F32)
    ahead = gather(groups[0])
    for i, ks in enumerate(groups):
        half = ahead
        if i + 1 < len(groups):
            ahead = gather(groups[i + 1])
        y = mm(half_silu(half.reshape(len(ks) * rows, width)), w2)
        scale = inverse_norm(y).reshape(len(ks), rows, 1)
        y = y.reshape(len(ks), rows, width)
        for j, k in enumerate(ks):
            live = (places[:, k : k + 1] >= 0).astype(F32)
            total = total + y[j] * (scale[j] * live)
    return total * (1.0 + vectors[1:2, :])


def begin(places, pieces, block, slots):
    count, degree = places.shape
    width = pieces[0].shape[1]
    table_rows = sum(p.shape[0] for p in pieces)

    def body(places, *refs):
        *pieces_in, out, table = refs
        lay(pieces_in, table)
        lanes = lax.broadcasted_iota(I32, (block, table_rows), 1)
        for at in range(0, count, block):
            near = places[pl.ds(at, block), :]
            for k in range(0, degree, slots):
                ks = range(k, min(k + slots, degree))
                picked = mm(chosen(near, ks, lanes), table[...])
                out[pl.ds(at * degree + k * block, len(ks) * block), :] = picked.astype(BF)

    return launch(
        body, "begin", [places] + pieces, [SDS((count * degree, width), BF)], [((table_rows, width), BF)], 0,
        2 * count * degree * table_rows * width, 4 << 20,
    )[0]


def lay(pieces, table):
    start = 0
    for piece in pieces:
        table[pl.ds(start, piece.shape[0]), :] = piece[...]
        start += piece.shape[0]


def node_update(x, summed, w0, w1, w2, vectors):
    half = (mm(x, w0) + mm(summed.astype(BF), w1) + vectors[0:1, :]) * 0.5
    y = mm(half_silu(half), w2)
    return (x.astype(F32) + y * inverse_norm(y) * (1.0 + vectors[1:2, :])).astype(BF)


def rows_of(refs, at, count):
    picked = []
    start = 0
    for ref in refs:
        low, high = max(at - start, 0), min(at + count - start, ref.shape[0])
        if low < high:
            picked.append(ref[pl.ds(low, high - low), :])
        start += ref.shape[0]
    return picked[0] if len(picked) == 1 else jnp.concatenate(picked, axis=0)


def mesh_stage(xs, places, base_place, at, count, pieces, keep, bases, ew2, ev, nw, nw2, nv, following, fv, joined, steps, name, lift=0, begun=None):
    width = xs[0].shape[1]
    degree = places.shape[1]
    table_rows = sum(p.shape[0] for p in pieces)
    groups = [xs, bases, pieces, [places, ew2, ev, nw, nw2, nv, following], [] if fv is None else [fv], joined, [] if begun is None else [begun]]
    ins = [x for group in groups for x in group]
    rows_out = count + sum(x.shape[0] for x in joined)
    outs = [SDS((rows_out, width), BF), SDS((count, width), BF)]
    outs += [] if fv is None else [SDS((count, width), F32)]
    outs += [SDS((table_rows, width), BF)] if keep else []

    def body(*refs):
        refs = list(refs)
        taken = []
        for group in groups:
            taken.append(refs[: len(group)])
            refs = refs[len(group) :]
        xs, bases, pieces_in, (places, ew2, ev, nw, nw2, nv, follow), fv, joined_in, begun_in = taken
        table = pieces_in[0]
        if keep:
            table = refs[-1]
            lay(pieces_in, table)
        summed = edge_sum(places[pl.ds(base_place + at, count), :], degree, table, rows_of(bases, at, count), ew2[...], ev, steps, lift, *[(ref, at * degree) for ref in begun_in])
        new = node_update(rows_of(xs, at, count), summed, nw[0], nw[1], nw2[...], nv)
        refs[0][pl.ds(rows_out - count, count), :] = new
        start = 0
        for ref in joined_in:
            refs[0][pl.ds(start, ref.shape[0]), :] = ref[...]
            start += ref.shape[0]
        refs[1][...] = (mm(new, follow[0]) * 0.5).astype(BF)
        for ref in fv:
            refs[2][...] = (mm(new, follow[1]) + ref[0:1, :]) * 0.5

    flops = count * degree * (2 * width * table_rows + 2 * width * width)
    return launch(body, name, ins, outs, [], 0, flops, 6 << 20)


def decode_stage(x, places, degree, pieces, base, ew2, ev, nw, nw2, nv, block):
    rows, width = x.shape
    table_rows = sum(p.shape[0] for p in pieces)
    ins = [x, places, base, ew2, ev, nw, nw2, nv] + pieces
    outs = [SDS((rows, width), BF)]

    def body(*refs):
        refs = list(refs)
        x, places, base, ew2, ev, nw, nw2, nv = refs[:8]
        pieces_in = refs[8 : 8 + len(pieces)]
        out, table, new, sems = refs[8 + len(pieces) :]
        mover = Mover(sems)
        lay(pieces_in, table)
        tails = []
        for at in range(0, rows, block):
            part = pl.ds(at, block)
            summed = edge_sum(places[part, :], degree, table, base[part, :], ew2[...], ev, degree)
            new[part, :] = node_update(x[part, :], summed, nw[0], nw[1], nw2[...], nv)
            tails.append(mover.start(new.at[part], out.at[part]))
        for tail in tails:
            tail.wait()

    flops = rows * degree * (2 * width * table_rows + 2 * width * width)
    scratch = [((table_rows, width), BF), ((rows, width), BF)]
    return launch(body, "decode", ins, outs, scratch, rows // block, flops, 6 << 20, far_outs=(0,))[0]


def sender(size_x, size_y):
    def send(rows, move):
        pairs = []
        for i in range(size_x):
            for j in range(size_y):
                a, b = move(i, j)
                pairs.append((i * size_y + j, (a % size_x) * size_y + b % size_y))
        return lax.ppermute(rows, AXES, pairs)

    return send


def next_pair(i):
    return i + 1 if i % 2 else i - 1


def per_device(
    grid_latent, mesh_latent, encode_senders, mesh_senders, decode_senders,
    encoder_edges, encoder_edgebias, encoder_nodes, encoder_nodebias,
    process_edges, process_edgebias, process_nodes, process_nodebias,
    decoder_edges, decoder_edgebias, decoder_nodes, decoder_nodebias,
):
    grid_rows, width = grid_latent.shape
    mesh_rows = mesh_latent.shape[0]
    grid_border = grid_rows // 4
    mesh_border = mesh_rows // 4
    size_x = lax.axis_size("gx")
    size_y = lax.axis_size("gy")
    square = 2 * width * width
    send = sender(size_x, size_y)
    pair_x = lambda i, j: (i ^ 1, j)
    next_x = lambda i, j: (next_pair(i), j)
    pair_y = lambda i, j: (i, j ^ 1)
    next_y = lambda i, j: (i, next_pair(j))

    border = launch(
        border_kernel, "project_border", [grid_latent, encoder_edges], [SDS((grid_border, width), BF)],
        [((grid_border, width), BF), ((width, width), BF)], 5, grid_border * square, 1 << 20, far_ins=(0, 1),
    )[0]
    e = send(border, pair_x)
    o = send(border, next_x)
    z = send(border, next_y)
    c = send(border, pair_y)

    degrees = [ids.shape[0] + -ids.shape[0] % 8 for ids in (encode_senders, mesh_senders, decode_senders)]
    square_shape = ((width, width), BF)
    outs = [
        ((grid_rows, width), BF), ((mesh_rows, width), BF), ((grid_rows, width), BF),
        ((mesh_rows, width), F32), ((grid_rows, width), F32),
        ((mesh_rows, degrees[0]), I32), ((mesh_rows, degrees[1]), I32), ((grid_rows, degrees[2]), I32),
    ] + [square_shape] * 6 + [((2, width, width), BF)] * 5
    (
        grid_latent, mesh_latent, own, base, grid_base, encode_at, mesh_at, decode_at,
        ee2, en2, pe2, pn2, de2, dn2, en01, pe01, pn01, de01, dn01,
    ) = launch(
        functools.partial(prepare_kernel, (size_x, size_y), (grid_rows, mesh_rows, grid_border, mesh_border)), "prepare",
        [
            grid_latent, mesh_latent, encode_senders, mesh_senders, decode_senders, encoder_edges, encoder_nodes,
            process_edges, process_nodes, decoder_edges, decoder_nodes, encoder_edgebias, decoder_edgebias,
        ],
        [SDS(s, d) for s, d in outs],
        [
            (encode_senders.shape, I32), (mesh_senders.shape, I32), (decode_senders.shape, I32), square_shape, square_shape,
            ((2, width), F32), ((2, width), F32), ((6, width, width), BF),
        ],
        20, 2 * grid_rows * square, 12 << 20, far_ins=range(13), mib=16,
    )
    e, o, z, own = lax.optimization_barrier((e, o, z, own))
    ec = send(e, pair_y)
    oc = send(o, pair_y)
    ez = send(z, pair_x)
    oz = send(z, next_x)
    begun = begin(encode_at, [own, c, z, e, o], mesh_border, 8)
    lift = grid_rows + 4 * grid_border
    pieces = [ec, ez, oc, oz]

    cuts = list(range(0, mesh_rows + 1, mesh_border))
    encoded = []
    for at, end in zip(cuts, cuts[1:]):
        part = mesh_stage(
            [mesh_latent], encode_at, 0, at, end - at, pieces, at == 0, [base], ee2, encoder_edgebias, en01, en2,
            encoder_nodebias, pe01, process_edgebias, [], 8, "encode", lift, begun,
        )
        if at == 0:
            pieces = [part[3]]
        encoded.append(part)

    border = encoded[0][1]
    c = send(border, pair_y)
    z = send(border, next_y)
    column = glue((border, CM), (c, CM))
    step = 2
    while step < size_y:
        flip = 2 * step - 1
        other = send(column, lambda i, j, flip=flip: (i, j ^ flip))
        column = glue((column, CM * step), (other, CM * step))
        step *= 2
    stack = glue((border, mesh_border), (c, mesh_border), (z, mesh_border), (column, CM * size_y))
    e = send(stack, pair_x)
    o = send(stack, next_x)
    far = [send(column, lambda i, j, d=d: (i - d, j)) for d in range(2, size_x - 1)]
    pieces = [part[1] for part in encoded] + [c, z, e, o, column] + far

    first = mesh_stage(
        [encoded[0][0]], mesh_at, 0, 0, mesh_border, pieces, True, [encoded[0][2]], pe2, process_edgebias, pn01, pn2,
        process_nodebias, de01, None, [], 8, "process",
    )
    border = first[1]
    c = send(border, pair_y)
    z = send(border, next_y)
    half = (mesh_rows - mesh_border) // 2
    xs, bases = ([part[i] for part in encoded[1:]] for i in (0, 2))
    tables, joined = [first[2]], [first[0]]
    projected = [border]
    for at in (0, half):
        part = mesh_stage(
            xs, mesh_at, mesh_border, at, half, tables, False, bases, pe2, process_edgebias, pn01, pn2, process_nodebias, de01, None,
            joined if at else [], 4, "process",
        )
        joined.append(part[0])
        projected.append(part[1])
        if at == 0:
            c, z, joined[-1] = lax.optimization_barrier((c, z, joined[-1]))
    processed = joined[-1]
    stack = glue((border, mesh_border), (c, mesh_border), (z, mesh_border))
    e = send(stack, pair_x)
    o = send(stack, next_x)
    decoded = decode_stage(
        grid_latent, decode_at, decode_senders.shape[0], projected + [c, z, e, o], grid_base, de2, decoder_edgebias,
        dn01, dn2, decoder_nodebias, 128,
    )
    return (decoded, processed)


def solution(mesh):
    rows = P(AXES, None)
    senders = P(None, AXES)
    return jax.shard_map(
        per_device,
        mesh=mesh,
        in_specs=(rows, rows, senders, senders, senders) + (P(),) * 12,
        out_specs=(rows, rows),
        check_vma=False,
    )
```

```python
import functools

import jax
import jax.numpy as jnp
from jax import lax
from jax.experimental import pallas as pl
from jax.experimental.pallas import tpu as pltpu
from jax.sharding import PartitionSpec as P

AXES = ("gx", "gy")
CM = 4
EPS = 1e-05
BF = jnp.bfloat16
F32 = jnp.float32
I32 = jnp.int32
SDS = jax.ShapeDtypeStruct


def mm(a, b):
    return jnp.dot(a, b, preferred_element_type=F32)


def half_silu(half):
    return (half + half * jnp.tanh(half)).astype(BF)


def inverse_norm(centred):
    spread = jnp.mean(centred * centred, axis=-1, keepdims=True)
    return lax.rsqrt(spread + EPS)


def centre(w):
    w = w.astype(F32)
    return (w - jnp.mean(w, axis=-1, keepdims=True)).astype(BF)


class Mover:
    def __init__(self, sems):
        self.sems = sems
        self.used = 0

    def start(self, source, target):
        copy = pltpu.make_async_copy(source, target, self.sems.at[self.used])
        self.used += 1
        copy.start()
        return copy


def launch(body, name, ins, outs, scratch, copies, flops, nbytes, far_ins=(), far_outs=(), mib=10):
    near = pl.BlockSpec(memory_space=pltpu.VMEM)
    far = pl.BlockSpec(memory_space=pltpu.HBM)
    sems = [pltpu.SemaphoreType.DMA((copies,))] if copies else []
    ins = [pltpu.with_memory_space_constraint(x, pltpu.HBM) if i in far_ins else x for i, x in enumerate(ins)]
    return pl.pallas_call(
        body,
        out_shape=outs,
        in_specs=[far if i in far_ins else near for i in range(len(ins))],
        out_specs=[far if i in far_outs else near for i in range(len(outs))],
        scratch_shapes=[pltpu.VMEM(s, d) for s, d in scratch] + sems,
        compiler_params=pltpu.CompilerParams(vmem_limit_bytes=mib << 20),
        cost_estimate=pl.CostEstimate(flops=flops, bytes_accessed=nbytes, transcendentals=0),
        name=name,
    )(*ins)


def glue(parts, size_y=0):
    flat = [p for part in parts for p in ([q for _, q in part] if isinstance(part, list) else [part])]
    total = sum((part[0][1] if isinstance(part, list) else part)[2] for part in parts)
    width = flat[0][0].shape[1]

    def body(*refs):
        refs = list(refs)
        out = refs.pop()
        values = []
        for part in parts:
            if isinstance(part, list):
                place = lax.axis_index("gy")
                peer = jnp.where(place & 1 == 1, place + 1, place - 1)
                peer = jnp.where(peer < 0, peer + size_y, jnp.where(peer >= size_y, peer - size_y, peer))
                value = None
                for flip, (_, start, rows) in part:
                    option = refs.pop(0)[pl.ds(start, rows), :].astype(F32)
                    value = option if value is None else jnp.where((place ^ peer) == flip, option, value)
                values.append(value)
            else:
                _, start, rows = part
                values.append(refs.pop(0)[pl.ds(start, rows), :].astype(F32))
        out[...] = jnp.concatenate(values, axis=0).astype(BF)

    return launch(body, "glue", [p[0] for p in flat], [SDS((total, width), BF)], [], 0, 1 << 10, 1 << 18, mib=2)[0]


def border_kernel(x, w, out, x_v, w_v, sems):
    mover = Mover(sems)
    quarter = w_v.shape[0] // 4
    loads = [mover.start(x.at[pl.ds(0, x_v.shape[0])], x_v)]
    for i in range(4):
        part = pl.ds(i * quarter, quarter)
        loads.append(mover.start(w.at[0, part], w_v.at[part]))
    for load in loads:
        load.wait()
    out[...] = (mm(x_v[...], w_v[...]) * 0.5).astype(BF)


def split(value, by):
    if by & (by - 1) == 0:
        return value >> (by.bit_length() - 1), value & (by - 1)
    return value // by, value % by


def locate(ids, rows, border, coarse, sizes, places, early=False):
    size_x, size_y = sizes
    place_x, place_y = places
    owner, offset = split(jnp.maximum(ids, 0), rows)
    owner_x, owner_y = split(owner, size_y)
    step_x = owner_x - place_x
    step_x = jnp.where(step_x < 0, step_x + size_x, step_x)
    step_y = owner_y - place_y
    step_y = jnp.where(step_y < 0, step_y + size_y, step_y)
    ahead_x, ahead_y = (place_x & 1) == 0, (place_y & 1) == 0
    pair_x = jnp.where(ahead_x, 1, size_x - 1)
    pair_y = jnp.where(ahead_y, 1, size_y - 1)
    kind_x = jnp.where(step_x == 0, 0, jnp.where(step_x == pair_x, 1, 2))
    kind_y = jnp.where(step_y == 0, 0, jnp.where(step_y == pair_y, 1, 2))
    near_x = (step_x <= 1) | (step_x == size_x - 1)
    near_y = (step_y <= 1) | (step_y == size_y - 1)
    group = 3 * border + coarse * size_y
    first = jnp.where(kind_x == 0, rows - border, rows + 2 * border + (kind_x - 1) * group)
    found = first + kind_y * border + offset
    if early:
        slot = jnp.where(kind_x == 0, kind_y - 1, jnp.where(kind_y == 0, kind_x + 1, 2 * kind_x + kind_y + 1))
        found = rows + slot * border + offset
    if coarse:
        flip = owner_y ^ place_y
        column = jnp.where(kind_x == 0, 0, 3 * border)
        far = first + column
        tail = rows + 2 * border + 2 * group
        far = jnp.where(kind_x == 0, tail, far)
        far = jnp.where(near_x, far, tail + (step_x - 1) * coarse * size_y)
        far = far + (flip ^ (flip >> 1)) * coarse + offset
        nearby = near_x & near_y & (offset < border)
        found = jnp.where(nearby, found, far)
    found = jnp.where((step_x == 0) & (step_y == 0), offset, found)
    return jnp.where(ids >= 0, found, -1)


def turned(found):
    degree, count = found.shape
    pad = -degree % 8
    if pad:
        found = jnp.concatenate([found, jnp.full((pad, count), -1, I32)], axis=0)
    return found.astype(F32).T.astype(I32)


def prepare_kernel(
    sizes, shapes,
    grid, mesh, eids, ee, en, pe, eb,
    grid_o, mesh_o, own, ebase, eat, ee2, en2, en01, pe01,
    eids_v, w0_v, w1_v, eb_v, w2_v, sems,
):
    mover = Mover(sems)
    grid_rows, _, grid_border, _ = shapes
    pairs = (
        (eids, eids_v), (grid, grid_o), (ee.at[0], w0_v), (mesh, mesh_o), (ee.at[1], w1_v), (eb, eb_v),
        (ee.at[2], w2_v.at[0]), (en.at[2], w2_v.at[1]), (en.at[pl.ds(0, 2)], en01), (pe.at[pl.ds(0, 2)], pe01),
    )
    loads = [mover.start(a, b) for a, b in pairs]
    places = (lax.axis_index("gx"), lax.axis_index("gy"))
    loads[0].wait()
    eat[...] = turned(locate(eids_v[...], grid_rows, grid_border, 0, sizes, places, True))
    for load in loads[1:3]:
        load.wait()
    own[...] = (mm(grid_o[...], w0_v[...]) * 0.5).astype(BF)
    for load in loads[3:6]:
        load.wait()
    ebase[...] = (mm(mesh_o[...], w1_v[...]) + eb_v[0:1, :]) * 0.5
    for i, out in enumerate((ee2, en2)):
        loads[6 + i].wait()
        out[...] = centre(w2_v[i])
    for load in loads[8:]:
        load.wait()


def prepare_later_kernel(
    sizes, shapes,
    mids, dids, pe, pn, de, dn, db, grid,
    dbase, mat, dat, pe2, pn2, de2, dn2, pn01, de01, dn01,
    mids_v, dids_v, db_v, w2_v, sems,
):
    mover = Mover(sems)
    _, mesh_rows, _, mesh_border = shapes
    pairs = (
        (mids, mids_v), (dids, dids_v), (db, db_v),
        (pe.at[2], w2_v.at[0]), (pn.at[2], w2_v.at[1]), (de.at[2], w2_v.at[2]), (dn.at[2], w2_v.at[3]),
        (de.at[pl.ds(0, 2)], de01), (pn.at[pl.ds(0, 2)], pn01), (dn.at[pl.ds(0, 2)], dn01),
    )
    loads = [mover.start(a, b) for a, b in pairs]
    places = (lax.axis_index("gx"), lax.axis_index("gy"))
    loads[0].wait()
    mat[...] = turned(locate(mids_v[...], mesh_rows, mesh_border, CM, sizes, places))
    loads[1].wait()
    dat[...] = turned(locate(dids_v[...], mesh_rows, mesh_border, 0, sizes, places))
    loads[2].wait()
    for i, out in enumerate((pe2, pn2, de2, dn2)):
        loads[3 + i].wait()
        out[...] = centre(w2_v[i])
    loads[7].wait()
    dbase[...] = (mm(grid[...], de01[1]) + db_v[0:1, :]) * 0.5
    for load in loads[8:]:
        load.wait()


def chosen(places, ks, lanes):
    return jnp.concatenate([(places[:, k : k + 1] == lanes).astype(F32).astype(BF) for k in ks], axis=0)


def edge_sum(places, degree, table, base, w2, vectors, slots, lift=0, begun=None):
    rows, width = base.shape
    lanes = lift + lax.broadcasted_iota(I32, (rows, table.shape[0]), 1)
    groups = [range(k, min(k + slots, degree)) for k in range(0, degree, slots)]

    def gather(ks):
        half = mm(chosen(places, ks, lanes), table[...])
        half = half.reshape(len(ks), rows, width)
        if begun is not None:
            ref, start = begun
            half = half + ref[pl.ds(ks[0], len(ks)), pl.ds(start, rows), :].astype(F32)
        return half + base[None]

    total = jnp.zeros((rows, width), F32)
    ahead = gather(groups[0])
    for i, ks in enumerate(groups):
        half = ahead
        if i + 1 < len(groups):
            ahead = gather(groups[i + 1])
        y = mm(half_silu(half.reshape(len(ks) * rows, width)), w2)
        scale = inverse_norm(y).reshape(len(ks), rows, 1)
        y = y.reshape(len(ks), rows, width)
        for j, k in enumerate(ks):
            live = (places[:, k : k + 1] >= 0).astype(F32)
            total = total + y[j] * (scale[j] * live)
    return total * (1.0 + vectors[1:2, :])


def begin(places, pieces, block, slots):
    count, degree = places.shape
    width = pieces[0].shape[1]
    table_rows = sum(p.shape[0] for p in pieces)

    def body(places, *refs):
        *pieces_in, out, table = refs
        lay(pieces_in, table)
        lanes = lax.broadcasted_iota(I32, (block, table_rows), 1)
        for at in range(0, count, block):
            near = places[pl.ds(at, block), :]
            for k in range(0, degree, slots):
                ks = range(k, min(k + slots, degree))
                picked = mm(chosen(near, ks, lanes), table[...]).astype(BF)
                out[pl.ds(k, len(ks)), pl.ds(at, block), :] = picked.reshape(len(ks), block, width)

    return launch(
        body, "begin", [places] + pieces, [SDS((degree, count, width), BF)], [((table_rows, width), BF)], 0,
        2 * count * degree * table_rows * width, 4 << 20,
    )[0]


def ranged(pieces):
    return [p if isinstance(p, tuple) else (p, 0, p.shape[0]) for p in pieces]


def lay(refs, table, pieces=None):
    at = 0
    for i, ref in enumerate(refs):
        start, rows = (0, ref.shape[0]) if pieces is None else pieces[i][1:]
        table[pl.ds(at, rows), :] = ref[pl.ds(start, rows), :]
        at += rows


def node_update(x, summed, w0, w1, w2, vectors):
    half = (mm(x, w0) + mm(summed.astype(BF), w1) + vectors[0:1, :]) * 0.5
    y = mm(half_silu(half), w2)
    return (x.astype(F32) + y * inverse_norm(y) * (1.0 + vectors[1:2, :])).astype(BF)


def rows_of(refs, at, count):
    picked = []
    start = 0
    for ref in refs:
        low, high = max(at - start, 0), min(at + count - start, ref.shape[0])
        if low < high:
            picked.append(ref[pl.ds(low, high - low), :])
        start += ref.shape[0]
    return picked[0] if len(picked) == 1 else jnp.concatenate(picked, axis=0)


def mesh_stage(xs, places, base_place, at, count, pieces, keep, bases, ew2, ev, nw, nw2, nv, following, fv, joined, steps, name, lift=0, begun=None):
    width = xs[0].shape[1]
    degree = places.shape[1]
    pieces = ranged(pieces)
    table_rows = sum(p[2] for p in pieces)
    groups = [xs, bases, [p[0] for p in pieces], [places, ew2, ev, nw, nw2, nv, following], [] if fv is None else [fv], joined, [] if begun is None else [begun]]
    ins = [x for group in groups for x in group]
    rows_out = count + sum(x.shape[0] for x in joined)
    outs = [SDS((rows_out, width), BF), SDS((count, width), BF)]
    outs += [] if fv is None else [SDS((count, width), F32)]
    outs += [SDS((table_rows, width), BF)] if keep else []

    def body(*refs):
        refs = list(refs)
        taken = []
        for group in groups:
            taken.append(refs[: len(group)])
            refs = refs[len(group) :]
        xs, bases, pieces_in, (places, ew2, ev, nw, nw2, nv, follow), fv, joined_in, begun_in = taken
        table = pieces_in[0]
        if keep:
            table = refs[-1]
            lay(pieces_in, table, pieces)
        summed = edge_sum(places[pl.ds(base_place + at, count), :], degree, table, rows_of(bases, at, count), ew2[...], ev, steps, lift, *[(ref, at) for ref in begun_in])
        new = node_update(rows_of(xs, at, count), summed, nw[0], nw[1], nw2[...], nv)
        refs[0][pl.ds(rows_out - count, count), :] = new
        start = 0
        for ref in joined_in:
            refs[0][pl.ds(start, ref.shape[0]), :] = ref[...]
            start += ref.shape[0]
        refs[1][...] = (mm(new, follow[0]) * 0.5).astype(BF)
        for ref in fv:
            refs[2][...] = (mm(new, follow[1]) + ref[0:1, :]) * 0.5

    flops = count * degree * (2 * width * table_rows + 2 * width * width)
    return launch(body, name, ins, outs, [], 0, flops, 6 << 20)


def edge_stage(places, first, at, count, table, bases, ew2, ev, slots, lift=0, begun=None):
    width = table.shape[1]
    degree = places.shape[1]
    groups = [bases, [places, table, ew2, ev], [] if begun is None else [begun]]

    def body(*refs):
        refs = list(refs)
        taken = []
        for group in groups:
            taken.append(refs[: len(group)])
            refs = refs[len(group) :]
        bases, (places, table, ew2, ev), begun_in = taken
        summed = edge_sum(
            places[pl.ds(first + at, count), :], degree, table, rows_of(bases, at, count), ew2[...], ev, slots, lift,
            *[(ref, first + at) for ref in begun_in],
        )
        refs[0][...] = summed.astype(BF)

    flops = count * degree * (2 * width * table.shape[0] + 2 * width * width)
    return launch(body, "edges", [x for g in groups for x in g], [SDS((count, width), BF)], [], 0, flops, 4 << 20)[0]


def node_stage(xs, at, sums, nw, nw2, nv, following, fv, joined):
    width = xs[0].shape[1]
    count = sum(x.shape[0] for x in sums)
    groups = [xs, sums, [nw, nw2, nv, following], [] if fv is None else [fv], joined]
    rows_out = count + sum(x.shape[0] for x in joined)
    outs = [SDS((rows_out, width), BF), SDS((count, width), BF)]
    outs += [] if fv is None else [SDS((count, width), F32)]

    def body(*refs):
        refs = list(refs)
        taken = []
        for group in groups:
            taken.append(refs[: len(group)])
            refs = refs[len(group) :]
        xs, sums, (nw, nw2, nv, follow), fv, joined_in = taken
        new = node_update(rows_of(xs, at, count), rows_of(sums, 0, count), nw[0], nw[1], nw2[...], nv)
        lay(joined_in, refs[0])
        refs[0][pl.ds(rows_out - count, count), :] = new
        refs[1][...] = (mm(new, follow[0]) * 0.5).astype(BF)
        for ref in fv:
            refs[2][...] = (mm(new, follow[1]) + ref[0:1, :]) * 0.5

    return launch(body, "nodes", [x for g in groups for x in g], outs, [], 0, 10 * count * width * width, 4 << 20)


def decode_stage(x, places, degree, pieces, base, ew2, ev, nw, nw2, nv, block):
    rows, width = x.shape
    pieces = ranged(pieces)
    table_rows = sum(p[2] for p in pieces)
    ins = [x, places, base, ew2, ev, nw, nw2, nv] + [p[0] for p in pieces]
    outs = [SDS((rows, width), BF)]

    def body(*refs):
        refs = list(refs)
        x, places, base, ew2, ev, nw, nw2, nv = refs[:8]
        pieces_in = refs[8 : 8 + len(pieces)]
        out, table, sums, new, sems = refs[8 + len(pieces) :]
        mover = Mover(sems)
        lay(pieces_in, table, pieces)
        tails = []
        for at in range(0, rows, block):
            part = pl.ds(at, block)
            summed = edge_sum(places[part, :], degree, table, base[part, :], ew2[...], ev, 1)
            sums[part, :] = summed.astype(BF)
        for at in range(0, rows, block):
            part = pl.ds(at, block)
            new[part, :] = node_update(x[part, :], sums[part, :], nw[0], nw[1], nw2[...], nv)
            tails.append(mover.start(new.at[part], out.at[part]))
        for tail in tails:
            tail.wait()

    flops = rows * degree * (2 * width * table_rows + 2 * width * width)
    scratch = [((table_rows, width), BF), ((rows, width), BF), ((rows, width), BF)]
    return launch(body, "decode", ins, outs, scratch, rows // block, flops, 6 << 20, far_outs=(0,))[0]


def sender(size_x, size_y):
    def send(rows, move):
        pairs = []
        for i in range(size_x):
            for j in range(size_y):
                a, b = move(i, j)
                pairs.append((i * size_y + j, (a % size_x) * size_y + b % size_y))
        return lax.ppermute(rows, AXES, pairs)

    return send


def next_pair(i):
    return i + 1 if i % 2 else i - 1


def per_device(
    grid_latent, mesh_latent, encode_senders, mesh_senders, decode_senders,
    encoder_edges, encoder_edgebias, encoder_nodes, encoder_nodebias,
    process_edges, process_edgebias, process_nodes, process_nodebias,
    decoder_edges, decoder_edgebias, decoder_nodes, decoder_nodebias,
):
    grid_rows, width = grid_latent.shape
    mesh_rows = mesh_latent.shape[0]
    grid_border = grid_rows // 4
    mesh_border = mesh_rows // 4
    size_x = lax.axis_size("gx")
    size_y = lax.axis_size("gy")
    square = 2 * width * width
    send = sender(size_x, size_y)
    pair_x = lambda i, j: (i ^ 1, j)
    next_x = lambda i, j: (next_pair(i), j)
    pair_y = lambda i, j: (i, j ^ 1)
    next_y = lambda i, j: (i, next_pair(j))

    border = launch(
        border_kernel, "project_border", [grid_latent, encoder_edges], [SDS((grid_border, width), BF)],
        [((grid_border, width), BF), ((width, width), BF)], 5, grid_border * square, 1 << 20, far_ins=(0, 1),
    )[0]
    e = send(border, pair_x)
    o = send(border, next_x)
    z = send(border, next_y)
    c = send(border, pair_y)

    degrees = [ids.shape[0] + -ids.shape[0] % 8 for ids in (encode_senders, mesh_senders, decode_senders)]
    square_shape = ((width, width), BF)
    pair_shape = ((2, width, width), BF)
    facts = ((size_x, size_y), (grid_rows, mesh_rows, grid_border, mesh_border))
    outs = [
        ((grid_rows, width), BF), ((mesh_rows, width), BF), ((grid_rows, width), BF), ((mesh_rows, width), F32),
        ((mesh_rows, degrees[0]), I32), square_shape, square_shape, pair_shape, pair_shape,
    ]
    grid_latent, mesh_latent, own, base, encode_at, ee2, en2, en01, pe01 = launch(
        functools.partial(prepare_kernel, *facts), "prepare",
        [grid_latent, mesh_latent, encode_senders, encoder_edges, encoder_nodes, process_edges, encoder_edgebias],
        [SDS(s, d) for s, d in outs],
        [(encode_senders.shape, I32), square_shape, square_shape, ((2, width), F32), pair_shape],
        10, grid_rows * square, 6 << 20, far_ins=range(7), mib=12,
    )
    e, o, z, own = lax.optimization_barrier((e, o, z, own))
    ec = send(e, pair_y)
    oc = send(o, pair_y)
    ez = send(z, pair_x)
    oz = send(z, next_x)
    begun = begin(encode_at, [own, c, z, e, o], mesh_border, 8)
    lift = grid_rows + 4 * grid_border
    pieces = [ec, ez, oc, oz]

    encoded = mesh_stage(
        [mesh_latent], encode_at, 0, 0, mesh_border, pieces, True, [base], ee2, encoder_edgebias, en01, en2,
        encoder_nodebias, pe01, process_edgebias, [], 8, "encode", lift, begun,
    )
    cuts = [mesh_rows * k // 8 for k in (2, 3, 4, 6, 8)]
    sums = [
        edge_stage(encode_at, 0, at, end - at, encoded[3], [base], ee2, encoder_edgebias, 256 // (end - at), lift, begun)
        for at, end in zip(cuts, cuts[1:])
    ]
    outs = [
        ((grid_rows, width), F32), ((mesh_rows, degrees[1]), I32), ((grid_rows, degrees[2]), I32),
    ] + [square_shape] * 4 + [pair_shape] * 3
    border = encoded[1]
    c = send(border, pair_y)
    c, sums[0] = lax.optimization_barrier((c, sums[0]))
    column = [(border, 0, CM), (c, 0, CM)]
    others = []
    step = 2
    while step < size_y:
        flip = 2 * step - 1
        other = send(glue([(border, 0, mesh_border)] + column), lambda i, j, flip=flip: (i, j ^ flip))
        if step == 2:
            other, sums[1] = lax.optimization_barrier((other, sums[1]))
        if step == 2:
            later_in, other = lax.optimization_barrier((grid_latent, other))
            later = list(launch(
                functools.partial(prepare_later_kernel, *facts), "prepare_later",
                [mesh_senders, decode_senders, process_edges, process_nodes, decoder_edges, decoder_nodes, decoder_edgebias, later_in],
                [SDS(s, d) for s, d in outs],
                [(mesh_senders.shape, I32), (decode_senders.shape, I32), ((2, width), F32), ((4, width, width), BF)],
                10, grid_rows * square, 6 << 20, far_ins=range(7), mib=12,
            ))
        if step == 4:
            other, sums[2], later[0] = lax.optimization_barrier((other, sums[2], later[0]))
        others.append((flip, (other, 0, mesh_border)))
        column = column + [(other, mesh_border, CM * step)]
        step *= 2
    stack = glue([(border, 0, mesh_border), (c, 0, mesh_border), others] + column, size_y)
    column = glue(column)
    e = send(stack, pair_x)
    o = send(stack, next_x)
    far = [send(column, lambda i, j, d=d: (i - d, j)) for d in range(2, size_x - 1)]
    rest = node_stage([mesh_latent], mesh_border, sums, en01, en2, encoder_nodebias, pe01, process_edgebias, [])
    pieces = [encoded[1], rest[1], (stack, mesh_border, 2 * mesh_border), e, o, column] + far
    grid_base, mesh_at, decode_at, pe2, pn2, de2, dn2, pn01, de01, dn01 = later

    first = mesh_stage(
        [encoded[0]], mesh_at, 0, 0, mesh_border, pieces, True, [encoded[2]], pe2, process_edgebias, pn01, pn2,
        process_nodebias, de01, None, [], 8, "process",
    )
    border = first[1]
    c = send(border, pair_y)
    z = send(border, next_y)
    half = (mesh_rows - mesh_border) // 2
    sums = [
        edge_stage(mesh_at, mesh_border, at, half, first[2], [rest[2]], pe2, process_edgebias, 4) for at in (0, half)
    ]
    c, z, sums[0] = lax.optimization_barrier((c, z, sums[0]))
    processed, projected = node_stage([rest[0]], 0, sums, pn01, pn2, process_nodebias, de01, None, [first[0]])
    stack = glue([(border, 0, mesh_border), (c, 0, mesh_border), (z, 0, mesh_border)])
    e = send(stack, pair_x)
    o = send(stack, next_x)
    decoded = decode_stage(
        grid_latent, decode_at, decode_senders.shape[0], [border, projected, (stack, mesh_border, 2 * mesh_border), e, o], grid_base, de2, decoder_edgebias,
        dn01, dn2, decoder_nodebias, grid_rows // 2,
    )
    return (decoded, processed)


def solution(mesh):
    rows = P(AXES, None)
    senders = P(None, AXES)
    return jax.shard_map(
        per_device,
        mesh=mesh,
        in_specs=(rows, rows, senders, senders, senders) + (P(),) * 12,
        out_specs=(rows, rows),
        check_vma=False,
    )
```

```python
import functools

import jax
import jax.numpy as jnp
from jax import lax
from jax.experimental import pallas as pl
from jax.experimental.pallas import tpu as pltpu
from jax.sharding import PartitionSpec as P

AXES = ("gx", "gy")
CM = 4
EPS = 1e-05
BF = jnp.bfloat16
F32 = jnp.float32
I32 = jnp.int32
SDS = jax.ShapeDtypeStruct


def mm(a, b):
    return jnp.dot(a, b, preferred_element_type=F32)


def half_silu(half):
    return (half + half * jnp.tanh(half)).astype(BF)


def inverse_norm(centred):
    spread = jnp.mean(centred * centred, axis=-1, keepdims=True)
    return lax.rsqrt(spread + EPS)


def centre(w):
    w = w.astype(F32)
    return (w - jnp.mean(w, axis=-1, keepdims=True)).astype(BF)


class Mover:
    def __init__(self, sems):
        self.sems = sems
        self.used = 0

    def start(self, source, target):
        copy = pltpu.make_async_copy(source, target, self.sems.at[self.used])
        self.used += 1
        copy.start()
        return copy


def launch(body, name, ins, outs, scratch, copies, flops, nbytes, far_ins=(), far_outs=(), mib=10):
    near = pl.BlockSpec(memory_space=pltpu.VMEM)
    far = pl.BlockSpec(memory_space=pltpu.HBM)
    sems = [pltpu.SemaphoreType.DMA((copies,))] if copies else []
    ins = [pltpu.with_memory_space_constraint(x, pltpu.HBM) if i in far_ins else x for i, x in enumerate(ins)]
    return pl.pallas_call(
        body,
        out_shape=outs,
        in_specs=[far if i in far_ins else near for i in range(len(ins))],
        out_specs=[far if i in far_outs else near for i in range(len(outs))],
        scratch_shapes=[pltpu.VMEM(s, d) for s, d in scratch] + sems,
        compiler_params=pltpu.CompilerParams(vmem_limit_bytes=mib << 20),
        cost_estimate=pl.CostEstimate(flops=flops, bytes_accessed=nbytes, transcendentals=0),
        name=name,
    )(*ins)


def glue(parts, size_y=0):
    flat = [p for part in parts for p in ([q for _, q in part] if isinstance(part, list) else [part])]
    total = sum((part[0][1] if isinstance(part, list) else part)[2] for part in parts)
    width = flat[0][0].shape[1]

    def body(*refs):
        refs = list(refs)
        out = refs.pop()
        values = []
        for part in parts:
            if isinstance(part, list):
                place = lax.axis_index("gy")
                peer = jnp.where(place & 1 == 1, place + 1, place - 1)
                peer = jnp.where(peer < 0, peer + size_y, jnp.where(peer >= size_y, peer - size_y, peer))
                value = None
                for flip, (_, start, rows) in part:
                    option = refs.pop(0)[pl.ds(start, rows), :].astype(F32)
                    value = option if value is None else jnp.where((place ^ peer) == flip, option, value)
                values.append(value)
            else:
                _, start, rows = part
                values.append(refs.pop(0)[pl.ds(start, rows), :].astype(F32))
        out[...] = jnp.concatenate(values, axis=0).astype(BF)

    return launch(body, "glue", [p[0] for p in flat], [SDS((total, width), BF)], [], 0, 1 << 10, 1 << 18, mib=2)[0]


def border_kernel(x, w, out, x_v, w_v, sems):
    mover = Mover(sems)
    quarter = w_v.shape[0] // 4
    loads = [mover.start(x.at[pl.ds(0, x_v.shape[0])], x_v)]
    for i in range(4):
        part = pl.ds(i * quarter, quarter)
        loads.append(mover.start(w.at[0, part], w_v.at[part]))
    for load in loads:
        load.wait()
    out[...] = (mm(x_v[...], w_v[...]) * 0.5).astype(BF)


def split(value, by):
    if by & (by - 1) == 0:
        return value >> (by.bit_length() - 1), value & (by - 1)
    return value // by, value % by


def locate(ids, rows, border, coarse, sizes, places, early=False):
    size_x, size_y = sizes
    place_x, place_y = places
    owner, offset = split(jnp.maximum(ids, 0), rows)
    owner_x, owner_y = split(owner, size_y)
    step_x = owner_x - place_x
    step_x = jnp.where(step_x < 0, step_x + size_x, step_x)
    step_y = owner_y - place_y
    step_y = jnp.where(step_y < 0, step_y + size_y, step_y)
    ahead_x, ahead_y = (place_x & 1) == 0, (place_y & 1) == 0
    pair_x = jnp.where(ahead_x, 1, size_x - 1)
    pair_y = jnp.where(ahead_y, 1, size_y - 1)
    kind_x = jnp.where(step_x == 0, 0, jnp.where(step_x == pair_x, 1, 2))
    kind_y = jnp.where(step_y == 0, 0, jnp.where(step_y == pair_y, 1, 2))
    near_x = (step_x <= 1) | (step_x == size_x - 1)
    near_y = (step_y <= 1) | (step_y == size_y - 1)
    line = coarse * size_y
    group = 3 * border + line
    tail = rows + 2 * border
    groups = tail + line * (size_x - 2)
    first = jnp.where(kind_x == 0, rows - border, groups + (kind_x - 1) * group)
    found = first + kind_y * border + offset
    if early:
        slot = jnp.where(kind_x == 0, kind_y - 1, jnp.where(kind_y == 0, kind_x + 1, 2 * kind_x + kind_y + 1))
        found = rows + slot * border + offset
    if coarse:
        flip = owner_y ^ place_y
        far = jnp.where(kind_x == 0, tail, first + 3 * border)
        far = jnp.where(near_x, far, tail + (step_x - 1) * line)
        index = jnp.where(flip & 1 == 1, 1 + (flip >> 1), jnp.where(flip == 0, 0, size_y // 2 + (flip >> 1)))
        far = far + index * coarse + offset
        nearby = near_x & near_y & (offset < border)
        found = jnp.where(nearby, found, far)
    found = jnp.where((step_x == 0) & (step_y == 0), offset, found)
    return jnp.where(ids >= 0, found, -1)


def turned(found):
    degree, count = found.shape
    pad = -degree % 8
    if pad:
        found = jnp.concatenate([found, jnp.full((pad, count), -1, I32)], axis=0)
    return found.astype(F32).T.astype(I32)


def prepare_kernel(
    sizes, shapes,
    grid, mesh, eids, ee, en, pe, eb, nb,
    grid_o, mesh_o, own, ebase, eself, eat, ee2, en2, en01, pe01,
    eids_v, w0_v, w1_v, eb_v, nb_v, w2_v, sems,
):
    mover = Mover(sems)
    grid_rows, _, grid_border, _ = shapes
    pairs = (
        (eids, eids_v), (grid, grid_o), (ee.at[0], w0_v), (mesh, mesh_o), (ee.at[1], w1_v), (eb, eb_v),
        (ee.at[2], w2_v.at[0]), (en.at[2], w2_v.at[1]), (nb, nb_v), (en.at[pl.ds(0, 2)], en01), (pe.at[pl.ds(0, 2)], pe01),
    )
    loads = [mover.start(a, b) for a, b in pairs]
    places = (lax.axis_index("gx"), lax.axis_index("gy"))
    loads[0].wait()
    eat[...] = turned(locate(eids_v[...], grid_rows, grid_border, 0, sizes, places, True))
    for load in loads[1:3]:
        load.wait()
    own[...] = (mm(grid_o[...], w0_v[...]) * 0.5).astype(BF)
    for load in loads[3:6]:
        load.wait()
    ebase[...] = (mm(mesh_o[...], w1_v[...]) + eb_v[0:1, :]) * 0.5
    for i, out in enumerate((ee2, en2)):
        loads[6 + i].wait()
        out[...] = centre(w2_v[i])
    for load in loads[8:]:
        load.wait()
    eself[...] = mm(mesh_o[...], en01[0]) + nb_v[0:1, :]


def prepare_mesh_kernel(
    sizes, shapes,
    mids, pe, pn, de,
    mat, pe2, pn2, pn01, de01,
    mids_v, w2_v, sems,
):
    mover = Mover(sems)
    _, mesh_rows, _, mesh_border = shapes
    pairs = (
        (mids, mids_v), (pe.at[2], w2_v.at[0]), (pn.at[2], w2_v.at[1]), (pn.at[pl.ds(0, 2)], pn01), (de.at[pl.ds(0, 2)], de01),
    )
    loads = [mover.start(a, b) for a, b in pairs]
    loads[0].wait()
    places = (lax.axis_index("gx"), lax.axis_index("gy"))
    mat[...] = turned(locate(mids_v[...], mesh_rows, mesh_border, CM, sizes, places))
    for i, out in enumerate((pe2, pn2)):
        loads[1 + i].wait()
        out[...] = centre(w2_v[i])
    for load in loads[3:]:
        load.wait()


def prepare_grid_kernel(
    sizes, shapes,
    dids, de, dn, db, nb, grid, de01,
    dbase, dself, dat, de2, dn2, dn01,
    dids_v, db_v, nb_v, w2_v, sems,
):
    mover = Mover(sems)
    _, mesh_rows, _, mesh_border = shapes
    pairs = (
        (dids, dids_v), (db, db_v), (nb, nb_v), (de.at[2], w2_v.at[0]), (dn.at[2], w2_v.at[1]), (dn.at[pl.ds(0, 2)], dn01),
    )
    loads = [mover.start(a, b) for a, b in pairs]
    loads[0].wait()
    places = (lax.axis_index("gx"), lax.axis_index("gy"))
    dat[...] = turned(locate(dids_v[...], mesh_rows, mesh_border, 0, sizes, places))
    for load in loads[1:3]:
        load.wait()
    dbase[...] = (mm(grid[...], de01[1]) + db_v[0:1, :]) * 0.5
    for i, out in enumerate((de2, dn2)):
        loads[3 + i].wait()
        out[...] = centre(w2_v[i])
    loads[5].wait()
    dself[...] = mm(grid[...], dn01[0]) + nb_v[0:1, :]


def chosen(places, ks, lanes):
    return jnp.concatenate([(places[:, k : k + 1] == lanes).astype(F32).astype(BF) for k in ks], axis=0)


def edge_sum(places, degree, table, base, w2, vectors, slots, lift=0, begun=None):
    rows, width = base.shape
    lanes = lift + lax.broadcasted_iota(I32, (rows, table.shape[0]), 1)
    groups = [range(k, min(k + slots, degree)) for k in range(0, degree, slots)]

    def gather(ks):
        half = mm(chosen(places, ks, lanes), table[...])
        half = half.reshape(len(ks), rows, width)
        if begun is not None:
            ref, start = begun
            half = half + ref[pl.ds(ks[0], len(ks)), pl.ds(start, rows), :].astype(F32)
        return half + base[None]

    total = jnp.zeros((rows, width), F32)
    ahead = gather(groups[0])
    for i, ks in enumerate(groups):
        half = ahead
        if i + 1 < len(groups):
            ahead = gather(groups[i + 1])
        y = mm(half_silu(half.reshape(len(ks) * rows, width)), w2)
        scale = inverse_norm(y).reshape(len(ks), rows, 1)
        y = y.reshape(len(ks), rows, width)
        for j, k in enumerate(ks):
            live = (places[:, k : k + 1] >= 0).astype(F32)
            total = total + y[j] * (scale[j] * live)
    return total * (1.0 + vectors[1:2, :])


def begin(places, pieces, block, slots, latents=(), ew=None, ev=None, nw=None, nv=None):
    count, degree = places.shape
    pieces = ranged(pieces)
    width = pieces[0][0].shape[1]
    table_rows = sum(p[2] for p in pieces)
    groups = [[p[0] for p in pieces], list(latents), [ew, ev, nw, nv] if latents else []]
    outs = [SDS((degree, count, width), BF)] + [SDS((count, width), F32)] * (2 if latents else 0)

    def body(places, *refs):
        (pieces_in, latents, extra), refs = taken(groups, refs)
        out, table = refs[0], refs[-1]
        lay(pieces_in, table, pieces)
        lanes = lax.broadcasted_iota(I32, (block, table_rows), 1)
        for at in range(0, count, block):
            near = places[pl.ds(at, block), :]
            for k in range(0, degree, slots):
                ks = range(k, min(k + slots, degree))
                picked = mm(chosen(near, ks, lanes), table[...]).astype(BF)
                out[pl.ds(k, len(ks)), pl.ds(at, block), :] = picked.reshape(len(ks), block, width)
        if latents:
            ew, ev, nw, nv = extra
            x = rows_of(latents, 0, count)
            refs[1][...] = (mm(x, ew[1]) + ev[0:1, :]) * 0.5
            refs[2][...] = mm(x, nw[0]) + nv[0:1, :]

    return launch(
        body, "begin", [places] + [x for g in groups for x in g], outs, [((table_rows, width), BF)], 0,
        2 * count * degree * table_rows * width, 4 << 20,
    )


def taken(groups, refs):
    refs = list(refs)
    split_refs = []
    for group in groups:
        split_refs.append(refs[: len(group)])
        refs = refs[len(group) :]
    return split_refs, refs


def ranged(pieces):
    return [p if isinstance(p, tuple) else (p, 0, p.shape[0]) for p in pieces]


def lay(refs, table, pieces=None):
    at = 0
    for i, ref in enumerate(refs):
        start, rows = (0, ref.shape[0]) if pieces is None else pieces[i][1:]
        table[pl.ds(at, rows), :] = ref[pl.ds(start, rows), :]
        at += rows


def node_update(x, own, summed, w1, w2, vectors):
    half = (own + mm(summed.astype(BF), w1)) * 0.5
    y = mm(half_silu(half), w2)
    return (x.astype(F32) + y * inverse_norm(y) * (1.0 + vectors[1:2, :])).astype(BF)


def rows_of(refs, at, count):
    picked = []
    start = 0
    for ref in refs:
        low, high = max(at - start, 0), min(at + count - start, ref.shape[0])
        if low < high:
            picked.append(ref[pl.ds(low, high - low), :])
        start += ref.shape[0]
    return picked[0] if len(picked) == 1 else jnp.concatenate(picked, axis=0)


def mesh_stage(x, own, places, count, pieces, base, ew2, ev, nw, nw2, nv, following, slots, name, lift, begun):
    width = x.shape[1]
    degree = places.shape[1]
    table_rows = sum(p.shape[0] for p in pieces)
    part = pl.ds(0, count)

    def body(x, own, places, base, ew2, ev, nw, nw2, nv, follow, begun, *refs):
        *pieces_in, new_o, proj, table = refs
        lay(pieces_in, table)
        summed = edge_sum(places[part, :], degree, table, base[part, :], ew2[...], ev, slots, lift, (begun, 0))
        new = node_update(x[part, :], own[part, :], summed, nw[1], nw2[...], nv)
        new_o[...] = new
        proj[...] = (mm(new, follow[0]) * 0.5).astype(BF)

    flops = count * degree * (2 * width * table_rows + 2 * width * width)
    outs = [SDS((count, width), BF), SDS((count, width), BF), SDS((table_rows, width), BF)]
    ins = [x, own, places, base, ew2, ev, nw, nw2, nv, following, begun] + pieces
    return launch(body, name, ins, outs, [], 0, flops, 6 << 20)


def edge_stage(places, at, count, table, base, ew2, ev, slots, lift, begun):
    width = table.shape[1]
    degree = places.shape[1]
    part = pl.ds(at, count)

    def body(places, table, base, ew2, ev, begun, out):
        summed = edge_sum(places[part, :], degree, table, base[part, :], ew2[...], ev, slots, lift, (begun, at))
        out[...] = summed.astype(BF)

    flops = count * degree * (2 * width * table.shape[0] + 2 * width * width)
    return launch(
        body, "edges", [places, table, base, ew2, ev, begun], [SDS((count, width), BF)], [], 0, flops, 4 << 20
    )[0]


def node_stage(xs, own, at, sums, nw, nw2, nv, following, joined=()):
    width = own.shape[1]
    count = sum(x.shape[0] for x in sums)
    groups = [xs, sums, [own, nw, nw2, nv, following], list(joined)]
    rows_out = count + sum(x.shape[0] for x in joined)
    outs = [SDS((rows_out, width), BF), SDS((count, width), BF)]
    x_at = at if xs[0].shape[0] > count else 0

    def body(*refs):
        (xs, sums, (own, nw, nw2, nv, follow), joined_in), (new_o, proj) = taken(groups, refs)
        new = node_update(
            rows_of(xs, x_at, count), own[pl.ds(at, count), :], rows_of(sums, 0, count), nw[1], nw2[...], nv
        )
        lay(joined_in, new_o)
        new_o[pl.ds(rows_out - count, count), :] = new
        proj[...] = (mm(new, follow[0]) * 0.5).astype(BF)

    return launch(body, "nodes", [x for g in groups for x in g], outs, [], 0, 10 * count * width * width, 4 << 20)


def decode_stage(x, own, places, degree, pieces, base, ew2, ev, nw, nw2, nv, passed, block):
    rows, width = x.shape
    pieces = ranged(pieces)
    table_rows = sum(p[2] for p in pieces)
    ins = [x, own, places, base, ew2, ev, nw, nw2, nv, passed] + [p[0] for p in pieces]
    outs = [SDS((rows, width), BF), SDS(passed.shape, BF)]

    def body(x, own, places, base, ew2, ev, nw, nw2, nv, passed, *refs):
        *pieces_in, out, passed_o, table, sums, new, sems = refs
        mover = Mover(sems)
        tails = [mover.start(passed, passed_o)]
        lay(pieces_in, table, pieces)
        for at in range(0, rows, block):
            part = pl.ds(at, block)
            summed = edge_sum(places[part, :], degree, table, base[part, :], ew2[...], ev, 1)
            sums[part, :] = summed.astype(BF)
        for at in range(0, rows, block):
            part = pl.ds(at, block)
            new[part, :] = node_update(x[part, :], own[part, :], sums[part, :], nw[1], nw2[...], nv)
            tails.append(mover.start(new.at[part], out.at[part]))
        for tail in tails:
            tail.wait()

    flops = rows * degree * (2 * width * table_rows + 2 * width * width)
    scratch = [((table_rows, width), BF), ((rows, width), BF), ((rows, width), BF)]
    return launch(body, "decode", ins, outs, scratch, 1 + rows // block, flops, 6 << 20, far_outs=(0, 1))


def sender(size_x, size_y):
    def send(rows, move):
        pairs = []
        for i in range(size_x):
            for j in range(size_y):
                a, b = move(i, j)
                pairs.append((i * size_y + j, (a % size_x) * size_y + b % size_y))
        return lax.ppermute(rows, AXES, pairs)

    return send


def next_pair(i):
    return i + 1 if i % 2 else i - 1


def per_device(
    grid_latent, mesh_latent, encode_senders, mesh_senders, decode_senders,
    encoder_edges, encoder_edgebias, encoder_nodes, encoder_nodebias,
    process_edges, process_edgebias, process_nodes, process_nodebias,
    decoder_edges, decoder_edgebias, decoder_nodes, decoder_nodebias,
):
    grid_rows, width = grid_latent.shape
    mesh_rows = mesh_latent.shape[0]
    grid_border = grid_rows // 4
    mesh_border = mesh_rows // 4
    size_x = lax.axis_size("gx")
    size_y = lax.axis_size("gy")
    square = 2 * width * width
    send = sender(size_x, size_y)
    pair_x = lambda i, j: (i ^ 1, j)
    next_x = lambda i, j: (next_pair(i), j)
    pair_y = lambda i, j: (i, j ^ 1)
    next_y = lambda i, j: (i, next_pair(j))

    border = launch(
        border_kernel, "project_border", [grid_latent, encoder_edges], [SDS((grid_border, width), BF)],
        [((grid_border, width), BF), ((width, width), BF)], 5, grid_border * square, 1 << 20, far_ins=(0, 1),
    )[0]
    e = send(border, pair_x)
    o = send(border, next_x)
    z = send(border, next_y)
    c = send(border, pair_y)

    degrees = [ids.shape[0] + -ids.shape[0] % 8 for ids in (encode_senders, mesh_senders, decode_senders)]
    square_shape = ((width, width), BF)
    pair_shape = ((2, width, width), BF)
    vectors_shape = ((2, width), F32)
    facts = ((size_x, size_y), (grid_rows, mesh_rows, grid_border, mesh_border))
    outs = [
        ((grid_rows, width), BF), ((mesh_rows, width), BF), ((grid_rows, width), BF), ((mesh_rows, width), F32),
        ((mesh_rows, width), F32), ((mesh_rows, degrees[0]), I32), square_shape, square_shape, pair_shape, pair_shape,
    ]
    grid_latent, mesh_latent, own, base, self_part, encode_at, ee2, en2, en01, pe01 = launch(
        functools.partial(prepare_kernel, *facts), "prepare",
        [
            grid_latent, mesh_latent, encode_senders, encoder_edges, encoder_nodes, process_edges, encoder_edgebias,
            encoder_nodebias,
        ],
        [SDS(s, d) for s, d in outs],
        [(encode_senders.shape, I32), square_shape, square_shape, vectors_shape, vectors_shape, pair_shape],
        11, grid_rows * square, 6 << 20, far_ins=range(8), mib=12,
    )
    outs = [((mesh_rows, degrees[1]), I32), square_shape, square_shape, pair_shape, pair_shape]
    mesh_at, pe2, pn2, pn01, de01 = launch(
        functools.partial(prepare_mesh_kernel, *facts), "prepare_mesh",
        [mesh_senders, process_edges, process_nodes, decoder_edges], [SDS(s, d) for s, d in outs],
        [(mesh_senders.shape, I32), pair_shape], 5, 1 << 20, 4 << 20, far_ins=range(4), mib=8,
    )
    e, o, z, own, mesh_at = lax.optimization_barrier((e, o, z, own, mesh_at))
    ec = send(e, pair_y)
    oc = send(o, pair_y)
    ez = send(z, pair_x)
    oz = send(o, next_y)
    begun = begin(encode_at, [own, c, z, e, o], mesh_border, 8)[0]
    lift = grid_rows + 4 * grid_border
    encoded, border, table = mesh_stage(
        mesh_latent, self_part, encode_at, mesh_border, [ec, ez, oc, oz], base, ee2, encoder_edgebias, en01, en2,
        encoder_nodebias, pe01, 8, "encode", lift, begun,
    )
    cuts = [mesh_rows * k // 8 for k in (2, 4, 5, 8)]
    sums = []

    def advance(arrived):
        at, end = cuts[len(sums)], cuts[len(sums) + 1]
        arrived, ready = lax.optimization_barrier((arrived, base))
        sums.append(
            edge_stage(encode_at, at, end - at, table, ready, ee2, encoder_edgebias, max(4, 256 // (end - at)), lift, begun)
        )
        return arrived

    direct = []
    for flip in reversed(range(3, size_y, 2)):
        rows = mesh_border if flip & (flip + 1) == 0 else CM
        sent = border if rows == mesh_border else glue([(border, 0, rows)])
        direct.append((flip, rows, send(sent, lambda i, j, flip=flip: (i, j ^ flip))))
    direct.reverse()
    c = send(border, pair_y)
    c = advance(c)
    heads = [(other, 0, CM) for _, _, other in direct]
    relay = glue(heads)
    relay, sums[0] = lax.optimization_barrier((relay, sums[0]))
    relayed = send(relay, pair_y)
    relay = advance(relay)
    relayed, sums[1] = lax.optimization_barrier((relayed, sums[1]))
    column = [(border, 0, CM), (c, 0, CM)] + heads + [(relayed, 0, CM * len(heads))]
    others = [(flip, (other, 0, mesh_border)) for flip, rows, other in direct if rows == mesh_border]
    stack = glue([(border, 0, mesh_border), (c, 0, mesh_border), others] + column, size_y)
    column = glue(column)
    e = send(stack, pair_x)
    o = send(stack, next_x)
    far = [send(column, lambda i, j, d=d: (i - d, j)) for d in range(2, size_x - 1)]
    while len(sums) < len(cuts) - 1:
        column = advance(column)
    rest, projected = node_stage([mesh_latent], self_part, mesh_border, sums, en01, en2, encoder_nodebias, pe01)
    near = [border, projected, (stack, mesh_border, 2 * mesh_border), column] + far
    begun, base, self_part = begin(
        mesh_at, near, mesh_border, 8, [encoded, rest], pe01, process_edgebias, pn01, process_nodebias
    )
    lift = mesh_rows + 2 * mesh_border + CM * size_y * (size_x - 2)
    first, border, table = mesh_stage(
        encoded, self_part, mesh_at, mesh_border, [e, o], base, pe2, process_edgebias, pn01, pn2, process_nodebias,
        de01, 8, "process", lift, begun,
    )
    c = send(border, pair_y)
    z = send(border, next_y)
    half = (mesh_rows - mesh_border) // 2
    sums = [
        edge_stage(mesh_at, at, half, table, base, pe2, process_edgebias, 4, lift, begun)
        for at in (mesh_border, mesh_border + half)
    ]
    c, z, sums[0] = lax.optimization_barrier((c, z, sums[0]))
    z, senders = lax.optimization_barrier((z, decode_senders))
    outs = [
        ((grid_rows, width), F32), ((grid_rows, width), F32), ((grid_rows, degrees[2]), I32),
        square_shape, square_shape, pair_shape,
    ]
    grid_base, grid_self, decode_at, de2, dn2, dn01 = launch(
        functools.partial(prepare_grid_kernel, *facts), "prepare_grid",
        [senders, decoder_edges, decoder_nodes, decoder_edgebias, decoder_nodebias, grid_latent, de01],
        [SDS(s, d) for s, d in outs],
        [(decode_senders.shape, I32), vectors_shape, vectors_shape, pair_shape],
        6, 2 * grid_rows * square, 4 << 20, far_ins=range(5), mib=10,
    )
    processed, projected = node_stage([rest], self_part, mesh_border, sums, pn01, pn2, process_nodebias, de01, [first])
    stack = glue([(border, 0, mesh_border), (c, 0, mesh_border), (z, 0, mesh_border)])
    e = send(stack, pair_x)
    o = send(stack, next_x)
    decoded, processed = decode_stage(
        grid_latent, grid_self, decode_at, decode_senders.shape[0],
        [border, projected, (stack, mesh_border, 2 * mesh_border), e, o], grid_base, de2, decoder_edgebias, dn01, dn2,
        decoder_nodebias, processed, grid_rows // 2,
    )
    return (decoded, processed)


def solution(mesh):
    rows = P(AXES, None)
    senders = P(None, AXES)
    return jax.shard_map(
        per_device,
        mesh=mesh,
        in_specs=(rows, rows, senders, senders, senders) + (P(),) * 12,
        out_specs=(rows, rows),
        check_vma=False,
    )
```

```python
import functools

import jax
import jax.numpy as jnp
from jax import lax
from jax.experimental import pallas as pl
from jax.experimental.pallas import tpu as pltpu
from jax.sharding import PartitionSpec as P

AXES = ("gx", "gy")
CM = 4
EPS = 1e-05
BF = jnp.bfloat16
F32 = jnp.float32
I32 = jnp.int32
SDS = jax.ShapeDtypeStruct


def mm(a, b):
    return jnp.dot(a, b, preferred_element_type=F32)


def half_silu(half):
    return (half + half * jnp.tanh(half)).astype(BF)


def half_silu_edges(half):
    half = half.astype(BF)
    return half + half * jnp.tanh(half)


def inverse_norm(centred):
    spread = jnp.mean(centred * centred, axis=-1, keepdims=True)
    return lax.rsqrt(spread + EPS)


def centre(w):
    w = w.astype(F32)
    return (w - jnp.mean(w, axis=-1, keepdims=True)).astype(BF)


class Mover:
    def __init__(self, sems):
        self.sems = sems
        self.used = 0

    def start(self, source, target):
        copy = pltpu.make_async_copy(source, target, self.sems.at[self.used])
        self.used += 1
        copy.start()
        return copy


def launch(body, name, ins, outs, scratch, copies, flops, nbytes, far_ins=(), far_outs=(), mib=10):
    near = pl.BlockSpec(memory_space=pltpu.VMEM)
    far = pl.BlockSpec(memory_space=pltpu.HBM)
    sems = [pltpu.SemaphoreType.DMA((copies,))] if copies else []
    ins = [pltpu.with_memory_space_constraint(x, pltpu.HBM) if i in far_ins else x for i, x in enumerate(ins)]
    return pl.pallas_call(
        body,
        out_shape=outs,
        in_specs=[far if i in far_ins else near for i in range(len(ins))],
        out_specs=[far if i in far_outs else near for i in range(len(outs))],
        scratch_shapes=[pltpu.VMEM(s, d) for s, d in scratch] + sems,
        compiler_params=pltpu.CompilerParams(vmem_limit_bytes=mib << 20),
        cost_estimate=pl.CostEstimate(flops=flops, bytes_accessed=nbytes, transcendentals=0),
        name=name,
    )(*ins)


def glue(parts, size_y=0):
    flat = [p for part in parts for p in ([q for _, q in part] if isinstance(part, list) else [part])]
    total = sum((part[0][1] if isinstance(part, list) else part)[2] for part in parts)
    width = flat[0][0].shape[1]

    def body(*refs):
        refs = list(refs)
        out = refs.pop()
        values = []
        for part in parts:
            if isinstance(part, list):
                place = lax.axis_index("gy")
                peer = jnp.where(place & 1 == 1, place + 1, place - 1)
                peer = jnp.where(peer < 0, peer + size_y, jnp.where(peer >= size_y, peer - size_y, peer))
                value = None
                for flip, (_, start, rows) in part:
                    option = refs.pop(0)[pl.ds(start, rows), :].astype(F32)
                    value = option if value is None else jnp.where((place ^ peer) == flip, option, value)
                values.append(value)
            else:
                _, start, rows = part
                values.append(refs.pop(0)[pl.ds(start, rows), :].astype(F32))
        out[...] = jnp.concatenate(values, axis=0).astype(BF)

    return launch(body, "glue", [p[0] for p in flat], [SDS((total, width), BF)], [], 0, 1 << 10, 1 << 18, mib=2)[0]


def border_kernel(x, w, out, x_v, w_v, sems):
    mover = Mover(sems)
    quarter = w_v.shape[0] // 4
    loads = [mover.start(x.at[pl.ds(0, x_v.shape[0])], x_v)]
    for i in range(4):
        part = pl.ds(i * quarter, quarter)
        loads.append(mover.start(w.at[0, part], w_v.at[part]))
    for load in loads:
        load.wait()
    out[...] = (mm(x_v[...], w_v[...]) * 0.5).astype(BF)


def split(value, by):
    if by & (by - 1) == 0:
        return value >> (by.bit_length() - 1), value & (by - 1)
    return value // by, value % by


def locate(ids, rows, border, coarse, sizes, places, early=False):
    size_x, size_y = sizes
    place_x, place_y = places
    owner, offset = split(jnp.maximum(ids, 0), rows)
    owner_x, owner_y = split(owner, size_y)
    step_x = owner_x - place_x
    step_x = jnp.where(step_x < 0, step_x + size_x, step_x)
    step_y = owner_y - place_y
    step_y = jnp.where(step_y < 0, step_y + size_y, step_y)
    ahead_x, ahead_y = (place_x & 1) == 0, (place_y & 1) == 0
    pair_x = jnp.where(ahead_x, 1, size_x - 1)
    pair_y = jnp.where(ahead_y, 1, size_y - 1)
    kind_x = jnp.where(step_x == 0, 0, jnp.where(step_x == pair_x, 1, 2))
    kind_y = jnp.where(step_y == 0, 0, jnp.where(step_y == pair_y, 1, 2))
    near_x = (step_x <= 1) | (step_x == size_x - 1)
    near_y = (step_y <= 1) | (step_y == size_y - 1)
    line = coarse * size_y
    group = 3 * border + line
    tail = rows + 2 * border
    groups = tail + line * (size_x - 2)
    first = jnp.where(kind_x == 0, rows - border, groups + (kind_x - 1) * group)
    found = first + kind_y * border + offset
    if early:
        slot = jnp.where(kind_x == 0, kind_y - 1, jnp.where(kind_y == 0, kind_x + 1, 2 * kind_x + kind_y + 1))
        found = rows + slot * border + offset
    if coarse:
        flip = owner_y ^ place_y
        far = jnp.where(kind_x == 0, tail, first + 3 * border)
        far = jnp.where(near_x, far, tail + (step_x - 1) * line)
        index = jnp.where(flip & 1 == 1, 1 + (flip >> 1), jnp.where(flip == 0, 0, size_y // 2 + (flip >> 1)))
        far = far + index * coarse + offset
        nearby = near_x & near_y & (offset < border)
        found = jnp.where(nearby, found, far)
    found = jnp.where((step_x == 0) & (step_y == 0), offset, found)
    return jnp.where(ids >= 0, found, -1)


def turned(found):
    degree, count = found.shape
    pad = -degree % 8
    if pad:
        found = jnp.concatenate([found, jnp.full((pad, count), -1, I32)], axis=0)
    return found.astype(F32).T.astype(I32)


def prepare_kernel(
    sizes, shapes,
    grid, mesh, eids, mids, ee, en, pe, pn, de, dn, eb, nb,
    grid_o, mesh_o, own, ebase, eself, eat, mat, ee2, en2, pe2, pn2, de2, dn2, en01, pe01, pn01, de01, dn01,
    eids_v, mids_v, w0_v, w1_v, eb_v, nb_v, w2_v, sems,
):
    mover = Mover(sems)
    grid_rows, mesh_rows, grid_border, mesh_border = shapes
    pairs = (
        (eids, eids_v), (mids, mids_v), (grid, grid_o), (ee.at[0], w0_v), (mesh, mesh_o), (ee.at[1], w1_v), (eb, eb_v),
        (ee.at[2], w2_v.at[0]), (en.at[2], w2_v.at[1]), (nb, nb_v), (pe.at[2], w2_v.at[2]), (pn.at[2], w2_v.at[3]), (de.at[2], w2_v.at[4]), (dn.at[2], w2_v.at[5]),
        (en.at[pl.ds(0, 2)], en01), (pe.at[pl.ds(0, 2)], pe01), (pn.at[pl.ds(0, 2)], pn01), (de.at[pl.ds(0, 2)], de01), (dn.at[pl.ds(0, 2)], dn01),
    )
    loads = [mover.start(a, b) for a, b in pairs]
    places = (lax.axis_index("gx"), lax.axis_index("gy"))
    loads[0].wait()
    eat[...] = turned(locate(eids_v[...], grid_rows, grid_border, 0, sizes, places, True))
    loads[1].wait()
    mat[...] = turned(locate(mids_v[...], mesh_rows, mesh_border, CM, sizes, places))
    for load in loads[2:4]:
        load.wait()
    own[...] = (mm(grid_o[...], w0_v[...]) * 0.5).astype(BF)
    for load in loads[4:7]:
        load.wait()
    ebase[...] = (mm(mesh_o[...], w1_v[...]) + eb_v[0:1, :]) * 0.5
    loads[9].wait()
    for i, out in enumerate((ee2, en2, pe2, pn2, de2, dn2)):
        loads[7 + i + (i > 1)].wait()
        out[...] = centre(w2_v[i])
    loads[14].wait()
    eself[...] = mm(mesh_o[...], en01[0]) + nb_v[0:1, :]
    for load in loads[15:]:
        load.wait()


def prepare_grid_kernel(sizes, shapes, dids, db, nb, grid, de01, dn01, dbase, dself, dat):
    _, mesh_rows, _, mesh_border = shapes
    places = (lax.axis_index("gx"), lax.axis_index("gy"))
    dat[...] = turned(locate(dids[...], mesh_rows, mesh_border, 0, sizes, places))
    dbase[...] = (mm(grid[...], de01[1]) + db[0:1, :]) * 0.5
    dself[...] = mm(grid[...], dn01[0]) + nb[0:1, :]


def chosen(places, ks, lanes):
    return jnp.concatenate([(places[:, k : k + 1] == lanes).astype(F32).astype(BF) for k in ks], axis=0)


def edge_sum(places, degree, table, base, w2, vectors, slots, lift=0, begun=None):
    rows, width = places.shape[0], table.shape[1]
    lanes = lift + lax.broadcasted_iota(I32, (rows, table.shape[0]), 1)
    groups = [range(k, min(k + slots, degree)) for k in range(0, degree, slots)]

    def gather(ks):
        half = mm(chosen(places, ks, lanes), table[...])
        half = half.reshape(len(ks), rows, width)
        if begun is None:
            return half + base[None]
        ref, start = begun
        return half + ref[pl.ds(ks[0], len(ks)), pl.ds(start, rows), :].astype(F32)

    total = jnp.zeros((rows, width), F32)
    ahead = gather(groups[0])
    for i, ks in enumerate(groups):
        half = ahead
        if i + 1 < len(groups):
            ahead = gather(groups[i + 1])
        y = mm(half_silu_edges(half.reshape(len(ks) * rows, width)), w2)
        scale = inverse_norm(y).reshape(len(ks), rows, 1)
        y = y.reshape(len(ks), rows, width)
        for j, k in enumerate(ks):
            live = (places[:, k : k + 1] >= 0).astype(F32)
            total = total + y[j] * (scale[j] * live)
    return total * (1.0 + vectors[1:2, :])


def begin(places, pieces, block, slots, base=None, latents=(), ew=None, ev=None, nw=None, nv=None):
    count, degree = places.shape
    pieces = ranged(pieces)
    width = pieces[0][0].shape[1]
    table_rows = sum(p[2] for p in pieces)
    groups = [[p[0] for p in pieces], list(latents), [ew, ev, nw, nv] if latents else [base]]
    outs = [SDS((degree, count, width), BF)] + [SDS((count, width), F32)] * (1 if latents else 0)

    def body(places, *refs):
        (pieces_in, latents, extra), refs = taken(groups, refs)
        out, table = refs[0], refs[-1]
        lay(pieces_in, table, pieces)
        if latents:
            ew, ev, nw, nv = extra
            x = rows_of(latents, 0, count)
            base = (mm(x, ew[1]) + ev[0:1, :]) * 0.5
            refs[1][...] = mm(x, nw[0]) + nv[0:1, :]
        else:
            base = extra[0][...]
        lanes = lax.broadcasted_iota(I32, (block, table_rows), 1)
        for at in range(0, count, block):
            near = places[pl.ds(at, block), :]
            for k in range(0, degree, slots):
                ks = range(k, min(k + slots, degree))
                picked = mm(chosen(near, ks, lanes), table[...]).reshape(len(ks), block, width)
                out[pl.ds(k, len(ks)), pl.ds(at, block), :] = (picked + base[at : at + block][None]).astype(BF)

    return launch(
        body, "begin", [places] + [x for g in groups for x in g], outs, [((table_rows, width), BF)], 0,
        2 * count * degree * table_rows * width, 4 << 20,
    )


def taken(groups, refs):
    refs = list(refs)
    split_refs = []
    for group in groups:
        split_refs.append(refs[: len(group)])
        refs = refs[len(group) :]
    return split_refs, refs


def ranged(pieces):
    return [p if isinstance(p, tuple) else (p, 0, p.shape[0]) for p in pieces]


def lay(refs, table, pieces=None):
    at = 0
    for i, ref in enumerate(refs):
        start, rows = (0, ref.shape[0]) if pieces is None else pieces[i][1:]
        table[pl.ds(at, rows), :] = ref[pl.ds(start, rows), :]
        at += rows


def node_update(x, own, summed, w1, w2, vectors):
    half = (own + mm(summed.astype(BF), w1)) * 0.5
    y = mm(half_silu(half), w2)
    return (x.astype(F32) + y * inverse_norm(y) * (1.0 + vectors[1:2, :])).astype(BF)


def rows_of(refs, at, count):
    picked = []
    start = 0
    for ref in refs:
        low, high = max(at - start, 0), min(at + count - start, ref.shape[0])
        if low < high:
            picked.append(ref[pl.ds(low, high - low), :])
        start += ref.shape[0]
    return picked[0] if len(picked) == 1 else jnp.concatenate(picked, axis=0)


def mesh_stage(x, own, places, count, pieces, ew2, ev, nw, nw2, nv, following, slots, name, lift, begun):
    width = x.shape[1]
    degree = places.shape[1]
    table_rows = sum(p.shape[0] for p in pieces)
    part = pl.ds(0, count)

    def body(x, own, places, ew2, ev, nw, nw2, nv, follow, begun, *refs):
        *pieces_in, new_o, proj, table = refs
        lay(pieces_in, table)
        summed = edge_sum(places[part, :], degree, table, None, ew2[...], ev, slots, lift, (begun, 0))
        new = node_update(x[part, :], own[part, :], summed, nw[1], nw2[...], nv)
        new_o[...] = new
        proj[...] = (mm(new, follow[0]) * 0.5).astype(BF)

    flops = count * degree * (2 * width * table_rows + 2 * width * width)
    outs = [SDS((count, width), BF), SDS((count, width), BF), SDS((table_rows, width), BF)]
    ins = [x, own, places, ew2, ev, nw, nw2, nv, following, begun] + pieces
    return launch(body, name, ins, outs, [], 0, flops, 6 << 20)


def edge_stage(places, at, count, table, ew2, ev, slots, lift, begun):
    width = table.shape[1]
    degree = places.shape[1]
    part = pl.ds(at, count)

    def body(places, table, ew2, ev, begun, out):
        summed = edge_sum(places[part, :], degree, table, None, ew2[...], ev, slots, lift, (begun, at))
        out[...] = summed.astype(BF)

    flops = count * degree * (2 * width * table.shape[0] + 2 * width * width)
    return launch(
        body, "edges", [places, table, ew2, ev, begun], [SDS((count, width), BF)], [], 0, flops, 4 << 20
    )[0]


def node_stage(xs, own, at, sums, nw, nw2, nv, following, joined=()):
    width = own.shape[1]
    count = sum(x.shape[0] for x in sums)
    groups = [xs, sums, [own, nw, nw2, nv, following], list(joined)]
    rows_out = count + sum(x.shape[0] for x in joined)
    outs = [SDS((rows_out, width), BF), SDS((count, width), BF)]
    x_at = at if xs[0].shape[0] > count else 0

    def body(*refs):
        (xs, sums, (own, nw, nw2, nv, follow), joined_in), (new_o, proj) = taken(groups, refs)
        new = node_update(
            rows_of(xs, x_at, count), own[pl.ds(at, count), :], rows_of(sums, 0, count), nw[1], nw2[...], nv
        )
        lay(joined_in, new_o)
        new_o[pl.ds(rows_out - count, count), :] = new
        proj[...] = (mm(new, follow[0]) * 0.5).astype(BF)

    return launch(body, "nodes", [x for g in groups for x in g], outs, [], 0, 10 * count * width * width, 4 << 20)


def decode_stage(x, own, places, degree, pieces, base, ew2, ev, nw, nw2, nv, passed, block):
    rows, width = x.shape
    pieces = ranged(pieces)
    table_rows = sum(p[2] for p in pieces)
    ins = [x, own, places, base, ew2, ev, nw, nw2, nv, passed] + [p[0] for p in pieces]
    outs = [SDS((rows, width), BF), SDS(passed.shape, BF)]

    def body(x, own, places, base, ew2, ev, nw, nw2, nv, passed, *refs):
        *pieces_in, out, passed_o, table, sums, new, sems = refs
        mover = Mover(sems)
        tails = [mover.start(passed, passed_o)]
        lay(pieces_in, table, pieces)
        for at in range(0, rows, block):
            part = pl.ds(at, block)
            summed = edge_sum(places[part, :], degree, table, base[part, :], ew2[...], ev, 1)
            sums[part, :] = summed.astype(BF)
        for at in range(0, rows, block):
            part = pl.ds(at, block)
            new[part, :] = node_update(x[part, :], own[part, :], sums[part, :], nw[1], nw2[...], nv)
            tails.append(mover.start(new.at[part], out.at[part]))
        for tail in tails:
            tail.wait()

    flops = rows * degree * (2 * width * table_rows + 2 * width * width)
    scratch = [((table_rows, width), BF), ((rows, width), BF), ((rows, width), BF)]
    return launch(body, "decode", ins, outs, scratch, 1 + rows // block, flops, 6 << 20, far_outs=(0, 1))


def sender(size_x, size_y):
    def send(rows, move):
        pairs = []
        for i in range(size_x):
            for j in range(size_y):
                a, b = move(i, j)
                pairs.append((i * size_y + j, (a % size_x) * size_y + b % size_y))
        return lax.ppermute(rows, AXES, pairs)

    return send


def next_pair(i):
    return i + 1 if i % 2 else i - 1


def per_device(
    grid_latent, mesh_latent, encode_senders, mesh_senders, decode_senders,
    encoder_edges, encoder_edgebias, encoder_nodes, encoder_nodebias,
    process_edges, process_edgebias, process_nodes, process_nodebias,
    decoder_edges, decoder_edgebias, decoder_nodes, decoder_nodebias,
):
    grid_rows, width = grid_latent.shape
    mesh_rows = mesh_latent.shape[0]
    grid_border = grid_rows // 4
    mesh_border = mesh_rows // 4
    size_x = lax.axis_size("gx")
    size_y = lax.axis_size("gy")
    square = 2 * width * width
    send = sender(size_x, size_y)
    pair_x = lambda i, j: (i ^ 1, j)
    next_x = lambda i, j: (next_pair(i), j)
    pair_y = lambda i, j: (i, j ^ 1)
    next_y = lambda i, j: (i, next_pair(j))

    border = launch(
        border_kernel, "project_border", [grid_latent, encoder_edges], [SDS((grid_border, width), BF)],
        [((grid_border, width), BF), ((width, width), BF)], 5, grid_border * square, 1 << 20, far_ins=(0, 1),
    )[0]
    e = send(border, pair_x)
    o = send(border, next_x)
    z = send(border, next_y)
    c = send(border, pair_y)

    degrees = [ids.shape[0] + -ids.shape[0] % 8 for ids in (encode_senders, mesh_senders, decode_senders)]
    square_shape = ((width, width), BF)
    pair_shape = ((2, width, width), BF)
    vectors_shape = ((2, width), F32)
    facts = ((size_x, size_y), (grid_rows, mesh_rows, grid_border, mesh_border))
    outs = [
        ((grid_rows, width), BF), ((mesh_rows, width), BF), ((grid_rows, width), BF), ((mesh_rows, width), F32),
        ((mesh_rows, width), F32), ((mesh_rows, degrees[0]), I32), ((mesh_rows, degrees[1]), I32),
    ] + [square_shape] * 6 + [pair_shape] * 5
    (
        grid_latent, mesh_latent, own, base, self_part, encode_at, mesh_at, ee2, en2, pe2, pn2, de2, dn2, en01, pe01,
        pn01, de01, dn01,
    ) = launch(
        functools.partial(prepare_kernel, *facts), "prepare",
        [
            grid_latent, mesh_latent, encode_senders, mesh_senders, encoder_edges, encoder_nodes, process_edges, process_nodes,
            decoder_edges, decoder_nodes, encoder_edgebias, encoder_nodebias,
        ],
        [SDS(s, d) for s, d in outs],
        [
            (encode_senders.shape, I32), (mesh_senders.shape, I32), square_shape, square_shape, vectors_shape, vectors_shape,
            ((6, width, width), BF),
        ],
        19, grid_rows * square, 6 << 20, far_ins=range(12), mib=20,
    )
    e, o, z, own = lax.optimization_barrier((e, o, z, own))
    ec = send(e, pair_y)
    oc = send(o, pair_y)
    ez = send(z, pair_x)
    oz = send(o, next_y)
    begun = begin(encode_at, [own, c, z, e, o], mesh_border, 8, base)[0]
    lift = grid_rows + 4 * grid_border
    encoded, border, table = mesh_stage(
        mesh_latent, self_part, encode_at, mesh_border, [ec, ez, oc, oz], ee2, encoder_edgebias, en01, en2,
        encoder_nodebias, pe01, 8, "encode", lift, begun,
    )
    cuts = [mesh_rows * k // 8 for k in (2, 4, 5, 8)]
    sums = []

    def advance(arrived):
        at, end = cuts[len(sums)], cuts[len(sums) + 1]
        arrived, ready = lax.optimization_barrier((arrived, encode_at))
        sums.append(
            edge_stage(ready, at, end - at, table, ee2, encoder_edgebias, max(4, 256 // (end - at)), lift, begun)
        )
        return arrived

    direct = []
    for flip in reversed(range(3, size_y, 2)):
        rows = mesh_border if flip & (flip + 1) == 0 else CM
        sent = border if rows == mesh_border else glue([(border, 0, rows)])
        direct.append((flip, rows, send(sent, lambda i, j, flip=flip: (i, j ^ flip))))
    direct.reverse()
    c = send(border, pair_y)
    c = advance(c)
    heads = [(other, 0, CM) for _, _, other in direct]
    relay = glue(heads)
    relay, sums[0] = lax.optimization_barrier((relay, sums[0]))
    relayed = send(relay, pair_y)
    relay = advance(relay)
    relayed, sums[1] = lax.optimization_barrier((relayed, sums[1]))
    column = [(border, 0, CM), (c, 0, CM)] + heads + [(relayed, 0, CM * len(heads))]
    others = [(flip, (other, 0, mesh_border)) for flip, rows, other in direct if rows == mesh_border]
    column = glue(column)
    stack = glue([(border, 0, mesh_border), (c, 0, mesh_border), others, (column, 0, CM * size_y)], size_y)
    far = [send(column, lambda i, j, d=d: (i - d, j)) for d in range(2, size_x - 1)]
    e = send(stack, pair_x)
    o = send(stack, next_x)
    while len(sums) < len(cuts) - 1:
        column = advance(column)
    rest, projected = node_stage([mesh_latent], self_part, mesh_border, sums, en01, en2, encoder_nodebias, pe01)
    near = [border, projected, (stack, mesh_border, 2 * mesh_border), column] + far
    begun, self_part = begin(
        mesh_at, near, mesh_border, 8, None, [encoded, rest], pe01, process_edgebias, pn01, process_nodebias
    )
    lift = mesh_rows + 2 * mesh_border + CM * size_y * (size_x - 2)
    first, border, table = mesh_stage(
        encoded, self_part, mesh_at, mesh_border, [e, o], pe2, process_edgebias, pn01, pn2, process_nodebias,
        de01, 8, "process", lift, begun,
    )
    c = send(border, pair_y)
    z = send(border, next_y)
    half = (mesh_rows - mesh_border) // 2
    sums = [
        edge_stage(mesh_at, at, half, table, pe2, process_edgebias, 4, lift, begun)
        for at in (mesh_border, mesh_border + half)
    ]
    c, z, sums[0] = lax.optimization_barrier((c, z, sums[0]))
    z, senders = lax.optimization_barrier((z, decode_senders))
    outs = [((grid_rows, width), F32), ((grid_rows, width), F32), ((grid_rows, degrees[2]), I32)]
    grid_base, grid_self, decode_at = launch(
        functools.partial(prepare_grid_kernel, *facts), "prepare_grid",
        [senders, decoder_edgebias, decoder_nodebias, grid_latent, de01, dn01],
        [SDS(s, d) for s, d in outs], [], 0, 2 * grid_rows * square, 4 << 20,
    )
    processed, projected = node_stage([rest], self_part, mesh_border, sums, pn01, pn2, process_nodebias, de01, [first])
    stack = glue([(border, 0, mesh_border), (c, 0, mesh_border), (z, 0, mesh_border)])
    e = send(stack, pair_x)
    o = send(stack, next_x)
    decoded, processed = decode_stage(
        grid_latent, grid_self, decode_at, decode_senders.shape[0],
        [border, projected, (stack, mesh_border, 2 * mesh_border), e, o], grid_base, de2, decoder_edgebias, dn01, dn2,
        decoder_nodebias, processed, grid_rows // 2,
    )
    return (decoded, processed)


def solution(mesh):
    rows = P(AXES, None)
    senders = P(None, AXES)
    return jax.shard_map(
        per_device,
        mesh=mesh,
        in_specs=(rows, rows, senders, senders, senders) + (P(),) * 12,
        out_specs=(rows, rows),
        check_vma=False,
    )
```
